32 devices in a mesh: row: 4 (over y, x), col: 8 (over z, core).
Axes of the slice: x: 2, y: 2, z: 4, core: 2. Of those that a mesh axis runs over, the one named last changes fastest.
Arguments:
- node_feats: bfloat16 [4096, 256], P(('row', 'col')), may hold values from -6 to 6
- degrees: int32 [4096], P(('row', 'col')), may hold values from 64 to 639
- self_weight: bfloat16 [256, 256], replicated, may hold values from -0.375 to 0.375
- neigh_weight: bfloat16 [256, 256], replicated, may hold values from -0.375 to 0.375
- bias: float32 [256], replicated, may hold values from -3 to 3
- tiles: bfloat16 [4, 8, 80, 128, 128], P('row', 'col'), may hold values from -6 to 6
- tile_rows: int32 [4, 8, 80], P('row', 'col'), may hold values from 0 to 7
- tile_cols: int32 [4, 8, 80], P('row', 'col'), may hold values from 0 to 3
- tile_counts: int32 [4, 8], P('row', 'col'), may hold values from 10 to 80, as said below
- out_grad: bfloat16 [4096, 256], P(('row', 'col')), may hold values from -6 to 6
Outputs:
- hidden: bfloat16 [4096, 256], P(('row', 'col'))
- feat_grad: bfloat16 [4096, 256], P(('row', 'col'))
- grad_self: float32 [256, 256], replicated
- grad_neigh: float32 [256, 256], replicated
- grad_bias: float32 [256], replicated
The draws below stay inside these ranges and needn't reach their ends.
Inputs may be any that keep to these rules, and one draw needn't show every extreme that they name: `tile_counts`: every grid row has a cell with all 80 slots holding blocks.
All inputs are finite; a program needn't handle non-finite values.
Results may differ from the reference program's by a relative error of at most 0.018.
Values may be sent and summed in bfloat16 or wider, within the bound.
No kernel may reach another device: no remote copies, remote signals or barrier semaphores. Data moves between devices by JAX's collectives and lax.ppermute only.
A program may use at most 64 MiB of HBM per device.

```python
import math
import jax
import jax.numpy as jnp
from jax import lax

F = 256
TILE = 128
ROWS_DEV = 128
KB = 80
NODES = 4096
ROW_BLOCKS = 8
COL_BLOCKS = 4
N_ROW = 4
N_COL = 8


def draw_tile_counts(key, part):
    first_key, second_key = jax.random.split(jax.random.fold_in(key, 7), 2)
    lowest = max(1, KB // 8)
    highest = max(lowest, KB // 2)
    base_counts = jax.random.randint(first_key, (N_ROW, N_COL), lowest, highest + 1)
    busiest = jax.random.randint(second_key, (N_ROW,), 0, N_COL)
    filled = jnp.arange(N_COL)[None, :] == busiest[:, None]
    return jnp.where(filled, KB, base_counts).astype(jnp.int32)


def plant(values, own_key, smallest, largest):
    extent = values.shape
    spot = [jax.random.randint(jax.random.fold_in(own_key, axis), (), 0, extent[axis]) for axis in range(len(extent))]
    values = values.at[tuple(spot)].set(smallest)
    longest = extent.index(max(extent))
    spot[longest] = (spot[longest] + 1) % extent[longest]
    return values.at[tuple(spot)].set(largest)


def block_levels(stream_key, extent, cuts, least, top_value):
    level = 1.0
    for dim, blocks in cuts:
        heights = jax.random.uniform(jax.random.fold_in(jax.random.fold_in(stream_key, 6), dim), (blocks,), jnp.float32, least / len(cuts), top_value / len(cuts))
        level = level * jnp.repeat(jnp.exp(heights), extent[dim] // blocks).reshape((-1,) + (1,) * (len(extent) - 1 - dim))
    return level


def bell_draw(key, extent, deviation, most, cuts=(), held_as=jnp.bfloat16):
    array = deviation * jax.random.normal(key, extent, jnp.float32)
    if cuts:
        array = array * block_levels(key, extent, cuts, -0.22, 0.18)
    return jnp.clip(array, -most, most).astype(held_as)


def setup_inputs(seed: int = 0) -> dict:
    arg_keys = jax.random.split(jax.random.key(seed), 11)
    return {
        "node_feats": bell_draw(arg_keys[0], (NODES, F), 1.0, 6.0, ((0, 32),)),
        "degrees": plant(jax.random.randint(arg_keys[1], (NODES,), 64, 640), jax.random.fold_in(arg_keys[1], 1), 64, 639).astype(jnp.int32),
        "self_weight": bell_draw(arg_keys[2], (F, F), F ** -0.5, 0.375),
        "neigh_weight": bell_draw(arg_keys[3], (F, F), F ** -0.5, 0.375),
        "bias": bell_draw(arg_keys[4], (F,), 0.5, 3.0, (), jnp.float32),
        "tiles": bell_draw(arg_keys[5], (N_ROW, N_COL, KB, TILE, TILE), 1.0, 6.0, ((0, 4), (1, 8))),
        "tile_rows": plant(jax.random.randint(arg_keys[6], (N_ROW, N_COL, KB), 0, ROW_BLOCKS), jax.random.fold_in(arg_keys[6], 1), 0, ROW_BLOCKS - 1).astype(jnp.int32),
        "tile_cols": plant(jax.random.randint(arg_keys[7], (N_ROW, N_COL, KB), 0, COL_BLOCKS), jax.random.fold_in(arg_keys[7], 1), 0, COL_BLOCKS - 1).astype(jnp.int32),
        "tile_counts": draw_tile_counts(jax.random.fold_in(arg_keys[10], 71), 0),
        "out_grad": bell_draw(arg_keys[9], (NODES, F), 1.0, 6.0, ((0, 32),)),
    }


def block_sum(block_vals, near_index, far_index, live_count, source, out_blocks, transposed):
    tile_edge = block_vals.shape[-1]
    feat_width = source.shape[-1]
    source_blocks = source.reshape(source.shape[0] // tile_edge, tile_edge, feat_width)
    picked = source_blocks[far_index].astype(jnp.float32)
    values = block_vals.astype(jnp.float32)
    if transposed:
        products = jnp.einsum('kab,kaf->kbf', values, picked)
    else:
        products = jnp.einsum('kab,kbf->kaf', values, picked)
    active = jnp.arange(block_vals.shape[0]) < live_count
    table = ((near_index[:, None] == jnp.arange(out_blocks)[None, :]) & active[:, None]).astype(jnp.float32)
    return jnp.einsum('kl,kaf->laf', table, products).reshape(out_blocks * tile_edge, feat_width)

def rounded_term(term):
    narrow = lax.optimization_barrier(term.astype(jnp.bfloat16))
    return narrow.astype(jnp.float32)

def reference(node_feats, degrees, self_weight, neigh_weight, bias, tiles, tile_rows, tile_cols, tile_counts, out_grad):
    per_device = ROWS_DEV
    feat_width = node_feats.shape[1]
    spanned = node_feats.reshape(N_ROW, N_COL, per_device, feat_width)
    col_stripes = spanned.transpose(1, 0, 2, 3).reshape(N_COL, N_ROW * per_device, feat_width)

    def forward_row(row_id):

        def add_pair(running, col_id):
            term = block_sum(tiles[row_id, col_id], tile_rows[row_id, col_id], tile_cols[row_id, col_id], tile_counts[row_id, col_id], col_stripes[col_id], ROW_BLOCKS, False)
            return (running + rounded_term(term), None)
        running, unused = lax.scan(add_pair, jnp.zeros((N_COL * per_device, feat_width), jnp.float32), jnp.arange(N_COL))
        return running
    summed = lax.map(forward_row, jnp.arange(N_ROW)).reshape(NODES, feat_width)
    degree_col = degrees.astype(jnp.float32)[:, None]
    aggregate = (summed / degree_col).astype(jnp.bfloat16)
    preact = jnp.dot(node_feats, self_weight, preferred_element_type=jnp.float32) + jnp.dot(aggregate, neigh_weight, preferred_element_type=jnp.float32) + bias.astype(jnp.float32)
    hidden = jax.nn.silu(preact).astype(jnp.bfloat16)
    sigmoid_val = jax.nn.sigmoid(preact)
    dpre = out_grad.astype(jnp.float32) * sigmoid_val * (1.0 + preact * (1.0 - sigmoid_val))
    dpre_b = dpre.astype(jnp.bfloat16)
    grad_scale = 1.0 / math.sqrt(NODES)
    first_dims = (((0,), (0,)), ((), ()))
    last_dims = (((1,), (1,)), ((), ()))
    grad_self = lax.dot_general(node_feats, dpre_b, first_dims, preferred_element_type=jnp.float32) * grad_scale
    grad_neigh = lax.dot_general(aggregate, dpre_b, first_dims, preferred_element_type=jnp.float32) * grad_scale
    grad_bias = lax.optimization_barrier(jnp.sum(dpre, axis=0)) * grad_scale
    back_agg = lax.dot_general(dpre_b, neigh_weight, last_dims, preferred_element_type=jnp.float32)
    spread = (back_agg / degree_col).astype(jnp.bfloat16)
    row_stripes = spread.reshape(N_ROW, N_COL * per_device, feat_width)

    def backward_col(col_id):

        def add_pair(running, row_id):
            term = block_sum(tiles[row_id, col_id], tile_cols[row_id, col_id], tile_rows[row_id, col_id], tile_counts[row_id, col_id], row_stripes[row_id], COL_BLOCKS, True)
            return (running + rounded_term(term), None)
        running, unused = lax.scan(add_pair, jnp.zeros((N_ROW * per_device, feat_width), jnp.float32), jnp.arange(N_ROW))
        return running
    gathered = lax.map(backward_col, jnp.arange(N_COL))
    neighbour_grad = gathered.reshape(N_COL, N_ROW, per_device, feat_width).transpose(1, 0, 2, 3).reshape(NODES, feat_width)
    own_grad = lax.dot_general(dpre_b, self_weight, last_dims, preferred_element_type=jnp.float32)
    feat_grad = (own_grad + neighbour_grad).astype(jnp.bfloat16)
    return (hidden, feat_grad, grad_self, grad_neigh, grad_bias)
```

```python
import functools
import math

import jax
import jax.numpy as jnp
from jax import lax
from jax.experimental import pallas as pl
from jax.experimental.pallas import tpu as pltpu
from jax.sharding import PartitionSpec as P

F32 = jnp.float32
BF16 = jnp.bfloat16
LAST = (((1,), (1,)), ((), ()))
FIRST = (((0,), (0,)), ((), ()))


def tile_products(block_vals, near_index, far_index, live_count, source, out_blocks, transposed):
    tile_total = block_vals.shape[0]
    group_size = min(16, tile_total)
    tile_edge = block_vals.shape[-1]
    feat_width = source.shape[-1]
    source_blocks = source.reshape(source.shape[0] // tile_edge, tile_edge, feat_width)
    turn_count = (live_count + group_size - 1) // group_size

    def advance(turn, running):
        first_tile = turn * group_size
        group_vals = lax.dynamic_slice_in_dim(block_vals, first_tile, group_size, 0)
        fetch_index = lax.dynamic_slice_in_dim(far_index, first_tile, group_size, 0)
        place_index = lax.dynamic_slice_in_dim(near_index, first_tile, group_size, 0)
        picked = source_blocks[fetch_index]
        if transposed:
            products = jnp.einsum("kab,kaf->kbf", group_vals, picked, preferred_element_type=F32)
        else:
            products = jnp.einsum("kab,kbf->kaf", group_vals, picked, preferred_element_type=F32)
        ordinal = first_tile + jnp.arange(group_size)
        active = ordinal < live_count
        table = (
            (place_index[:, None] == jnp.arange(out_blocks)[None, :]) & active[:, None]
        ).astype(F32)
        return running + jnp.einsum("kl,kaf->laf", table, products)

    initial = jnp.zeros((out_blocks, tile_edge, feat_width), F32)
    result = lax.fori_loop(0, turn_count, advance, initial)
    return result.reshape(out_blocks * tile_edge, feat_width)


def general_form(
    node_feats,
    degrees,
    self_weight,
    neigh_weight,
    bias,
    tiles,
    tile_rows,
    tile_cols,
    tile_counts,
    out_grad,
):
    grid_rows = lax.axis_size("row")
    grid_cols = lax.axis_size("col")
    per_device = node_feats.shape[0]
    tile_edge = tiles.shape[-1]
    block_vals = tiles[0, 0]
    block_rows = tile_rows[0, 0]
    block_cols = tile_cols[0, 0]
    live_count = tile_counts[0, 0]
    row_blocks = grid_cols * per_device // tile_edge
    col_blocks = grid_rows * per_device // tile_edge
    stripe = lax.all_gather(node_feats, "row", axis=0, tiled=True)
    partial_value = tile_products(
        block_vals, block_rows, block_cols, live_count, stripe, row_blocks, False
    )
    summed = lax.psum_scatter(
        partial_value.astype(BF16), "col", scatter_dimension=0, tiled=True
    ).astype(F32)
    degree_col = degrees.astype(F32)[:, None]
    aggregate = (summed / degree_col).astype(BF16)
    preact = (
        jnp.dot(node_feats, self_weight, preferred_element_type=F32)
        + jnp.dot(aggregate, neigh_weight, preferred_element_type=F32)
        + bias
    )
    hidden = jax.nn.silu(preact).astype(BF16)
    sigmoid_val = jax.nn.sigmoid(preact)
    dpre = out_grad.astype(F32) * sigmoid_val * (1.0 + preact * (1.0 - sigmoid_val))
    dpre_b = dpre.astype(BF16)
    self_term = lax.dot_general(node_feats, dpre_b, FIRST, preferred_element_type=F32)
    neigh_term = lax.dot_general(aggregate, dpre_b, FIRST, preferred_element_type=F32)
    bias_term = jnp.sum(dpre, axis=0)
    self_total, neigh_total, bias_total = lax.psum(
        (self_term, neigh_term, bias_term), ("row", "col")
    )
    grad_scale = 1.0 / math.sqrt(grid_rows * grid_cols * per_device)
    back_agg = lax.dot_general(dpre_b, neigh_weight, LAST, preferred_element_type=F32)
    spread = (back_agg / degree_col).astype(BF16)
    row_stripe = lax.all_gather(spread, "col", axis=0, tiled=True)
    back_partial = tile_products(
        block_vals, block_cols, block_rows, live_count, row_stripe, col_blocks, True
    )
    neighbour_grad = lax.psum_scatter(
        back_partial.astype(BF16), "row", scatter_dimension=0, tiled=True
    ).astype(F32)
    own_grad = lax.dot_general(dpre_b, self_weight, LAST, preferred_element_type=F32)
    feat_grad = (own_grad + neighbour_grad).astype(BF16)
    return (
        hidden,
        feat_grad,
        self_total * grad_scale,
        neigh_total * grad_scale,
        bias_total * grad_scale,
    )


def sds(shape, dtype):
    return jax.ShapeDtypeStruct(shape, dtype)


def call(body, outs, args, name, smem=0, scratch=(), cost=None, grid=None, in_specs=None):
    single = not isinstance(outs, (list, tuple))
    outs = [outs] if single else list(outs)
    if in_specs is None:
        in_specs = [pl.BlockSpec(memory_space=pltpu.SMEM)] * smem + [
            pl.BlockSpec(memory_space=pltpu.VMEM)
        ] * (len(args) - smem)
    flops, moved = cost or (1 << 20, 1 << 18)
    result = pl.pallas_call(
        body,
        out_shape=outs,
        in_specs=in_specs,
        out_specs=[pl.BlockSpec(memory_space=pltpu.VMEM)] * len(outs),
        scratch_shapes=list(scratch),
        compiler_params=pltpu.CompilerParams(vmem_limit_bytes=24 << 20),
        cost_estimate=pl.CostEstimate(flops=flops, bytes_accessed=moved, transcendentals=0),
        name=name,
    )(*args)
    return result[0] if single else result


def dot(a, b):
    return jnp.dot(a, b, preferred_element_type=F32)


def build_cell(place, tile_rows, tile_cols, tiles, grid_rows, grid_cols):
    total, edge = tiles.shape[0], tiles.shape[-1]
    group = 16 if total % 16 == 0 else total
    half = grid_cols // 2

    def body(place_ref, rows_ref, cols_ref, tiles_ref, cell_ref, sums):
        step = pl.program_id(0)

        @pl.when(step == 0)
        def _():
            sums[...] = jnp.zeros_like(sums)

        my_row, my_col, count = place_ref[0], place_ref[1], place_ref[2]
        first = step * group

        def add_tile(k, carry):
            near = rows_ref[first + k] ^ my_col
            far = cols_ref[first + k] ^ my_row
            slot = ((near >> 1) + half * (near & 1)) * grid_rows + far
            sums[slot] += tiles_ref[k].astype(F32)
            return carry

        lax.fori_loop(0, jnp.clip(count - first, 0, group), add_tile, 0)

        @pl.when(step == pl.num_programs(0) - 1)
        def _():
            for i in range(grid_cols):
                for j in range(grid_rows):
                    cell_ref[i * edge : (i + 1) * edge, j * edge : (j + 1) * edge] = sums[
                        i * grid_rows + j
                    ].astype(BF16)

    smem = pl.BlockSpec(memory_space=pltpu.SMEM)
    return pl.pallas_call(
        body,
        out_shape=sds((grid_cols * edge, grid_rows * edge), BF16),
        grid=(total // group,),
        in_specs=[smem] * 3 + [pl.BlockSpec((group, edge, edge), lambda i: (i, 0, 0))],
        out_specs=pl.BlockSpec((grid_cols * edge, grid_rows * edge), lambda i: (0, 0)),
        scratch_shapes=[pltpu.VMEM((grid_rows * grid_cols, edge, edge), F32)],
        compiler_params=pltpu.CompilerParams(vmem_limit_bytes=24 << 20),
        cost_estimate=pl.CostEstimate(
            flops=1 << 24, bytes_accessed=4 * total * edge * edge, transcendentals=0
        ),
        name="build_cell",
    )(place, tile_rows, tile_cols, tiles)


def swap(value, axis, distance):
    size = lax.axis_size(axis)
    return lax.ppermute(value, axis, [(i, i ^ distance) for i in range(size)])


def direct_form(
    node_feats,
    degrees,
    self_weight,
    neigh_weight,
    bias,
    tiles,
    tile_rows,
    tile_cols,
    tile_counts,
    out_grad,
):
    grid_rows = lax.axis_size("row")
    grid_cols = lax.axis_size("col")
    half = grid_cols // 2
    n, width = node_feats.shape
    grad_scale = 1.0 / math.sqrt(grid_rows * grid_cols * n)
    place = jnp.stack([lax.axis_index("row"), lax.axis_index("col"), tile_counts[0, 0]])

    feats = [node_feats] + [swap(node_feats, "row", k) for k in range(1, grid_rows)]

    cell = build_cell(place, tile_rows[0, 0], tile_cols[0, 0], tiles[0, 0], grid_rows, grid_cols)

    def prepare(x_ref, w_ref, b_ref, d_ref, pre_ref, deg_ref, degrow_ref):
        pre_ref[...] = dot(x_ref[...], w_ref[...]) + b_ref[...]
        line = d_ref[...].astype(F32)
        degrow_ref[...] = line
        deg_ref[...] = jnp.broadcast_to(line, (n, n)).T

    pre, deg, deg_row = call(
        prepare,
        [sds((n, width), F32), sds((n, n), F32), sds((1, n), F32)],
        [node_feats, self_weight, bias.reshape(1, width), degrees.reshape(1, n)],
        "prepare",
    )

    def products(part, cell_ref, *refs):
        *x_refs, out_ref = refs
        stripe = jnp.concatenate([r[...] for r in x_refs], axis=0)
        rows = half * n
        out_ref[...] = dot(cell_ref[part * rows : (part + 1) * rows, :], stripe).astype(
            out_ref.dtype
        )

    work = (2 * half * n * grid_rows * n * width, 1 << 20)
    sent = call(
        functools.partial(products, 1),
        sds((half * n, width), BF16),
        [cell, *feats],
        "forward_sent",
        cost=work,
    )
    sent_in = swap(sent, "col", 1)
    kept = call(
        functools.partial(products, 0),
        sds((half * n, width), F32),
        [cell, *feats],
        "forward_kept",
        cost=work,
    )

    def pair_sums(kept_ref, in_ref, own_ref, *out_refs):
        total = kept_ref[...] + in_ref[...].astype(F32)
        own_ref[...] = total[:n]
        for q, ref in enumerate(out_refs):
            ref[...] = total[(q + 1) * n : (q + 2) * n].astype(BF16)

    own_sum, *parts = call(
        pair_sums,
        [sds((n, width), F32)] + [sds((n, width), BF16)] * (half - 1),
        [kept, sent_in],
        "pair_sums",
    )
    parts_in = [swap(part, "col", 2 * (q + 1)) for q, part in enumerate(parts)]

    def dense(own_ref, *refs):
        *in_refs, pre_ref, deg_ref, degrow_ref, w_ref, g_ref, spread_ref, preact_ref, agg_ref = refs
        total = own_ref[...]
        for ref in in_refs:
            total = total + ref[...].astype(F32)
        d = deg_ref[...]
        agg = (total / jnp.concatenate([d] * (width // n), axis=1)).astype(BF16)
        agg_ref[...] = agg
        v = pre_ref[...] + dot(agg, w_ref[...])
        preact_ref[...] = v
        s = jax.nn.sigmoid(v)
        dpre = g_ref[...].astype(F32) * s * (1.0 + v * (1.0 - s))
        back = lax.dot_general(
            w_ref[...], dpre.astype(BF16), LAST, preferred_element_type=F32
        )
        spread_ref[...] = (back / degrow_ref[...]).astype(BF16)

    spread, preact, aggregate = call(
        dense,
        [sds((width, n), BF16), sds((n, width), F32), sds((n, width), BF16)],
        [own_sum, *parts_in, pre, deg, deg_row, neigh_weight, out_grad],
        "dense",
    )
    near = [spread] + [swap(spread, "col", 2 * q) for q in range(1, half)]

    pad = 16

    def terms(place_ref, v_ref, agg_ref, x_ref, w_ref, g_ref, hid_ref, own_ref, keep_ref, send_ref):
        v = v_ref[...]
        s = jax.nn.sigmoid(v)
        hid_ref[...] = (v * s).astype(BF16)
        dpre = g_ref[...].astype(F32) * s * (1.0 + v * (1.0 - s))
        dpre_b = dpre.astype(BF16)
        own_ref[...] = lax.dot_general(w_ref[...], dpre_b, LAST, preferred_element_type=F32)
        self_term = lax.dot_general(x_ref[...], dpre_b, FIRST, preferred_element_type=F32)
        neigh_term = lax.dot_general(agg_ref[...], dpre_b, FIRST, preferred_element_type=F32)
        first = (place_ref[1] & 1) == 0
        keep_ref[:width] = jnp.where(first, self_term, neigh_term).astype(BF16)
        send_ref[:width] = jnp.where(first, neigh_term, self_term).astype(BF16)
        line = jnp.broadcast_to(jnp.sum(dpre, axis=0, keepdims=True), (pad, width)).astype(BF16)
        keep_ref[width:] = line
        send_ref[width:] = line

    hidden, own_grad, g_keep, g_send = call(
        terms,
        [
            sds((n, width), BF16),
            sds((width, n), F32),
            sds((width + pad, width), BF16),
            sds((width + pad, width), BF16),
        ],
        [place, preact, aggregate, node_feats, self_weight, out_grad],
        "terms",
        smem=1,
    )
    g_in = swap(g_send, "col", 1)
    piece = width // 2

    def halves(place_ref, a_ref, b_ref, keep_ref, send_ref):
        x = place_ref[0] & 1
        mine = pl.ds(pl.multiple_of(x * piece, piece), piece)
        other = pl.ds(pl.multiple_of((1 - x) * piece, piece), piece)
        tail = pl.ds(width, pad)
        for ref, span in ((keep_ref, mine), (send_ref, other)):
            ref[:piece] = (a_ref[span, :].astype(F32) + b_ref[span, :].astype(F32)).astype(BF16)
            ref[piece:] = (a_ref[tail, :].astype(F32) + b_ref[tail, :].astype(F32)).astype(BF16)

    small = sds((piece + pad, width), BF16)
    h_keep, h_send = call(halves, [small, small], [place, g_keep, g_in], "halves", smem=1)
    h_in = swap(h_send, "row", 1)

    def add_two(a_ref, b_ref, out_ref):
        out_ref[...] = (a_ref[...].astype(F32) + b_ref[...].astype(F32)).astype(BF16)

    y_part = call(add_two, small, [h_keep, h_in], "add_x")
    for k in (2 ** i for i in range(1, grid_rows.bit_length() - 1)):
        y_part = call(add_two, small, [y_part, swap(y_part, "row", k)], "add_y")
    z_parts = [y_part] + [swap(y_part, "col", 2 * q) for q in range(1, half)]

    def add_many(*refs):
        *in_refs, out_ref = refs
        vals = [ref[...].astype(F32) for ref in in_refs]
        while len(vals) > 1:
            vals = [vals[i] + vals[i + 1] for i in range(0, len(vals), 2)]
        out_ref[...] = vals[0].astype(BF16)

    g_piece = call(add_many, small, z_parts, "add_z")
    g_other = swap(g_piece, "row", 1)

    far = [swap(part, "col", 1) for part in near]

    def back_first(cell_ref, *refs):
        *s_refs, out_ref = refs
        left = jnp.concatenate([r[...] for r in s_refs], axis=1)
        out_ref[...] = dot(left, cell_ref[: half * n, :])

    back_a = call(
        back_first, sds((width, grid_rows * n), F32), [cell, *near], "back_first", cost=work
    )

    def back_second(cell_ref, a_ref, base_ref, *refs):
        s_refs, out_refs = refs[:half], refs[half:]
        left = jnp.concatenate([r[...] for r in s_refs], axis=1)
        total = a_ref[...] + dot(left, cell_ref[half * n :, :])
        out_refs[0][...] = total[:, :n] + base_ref[...]
        for k in range(1, grid_rows):
            out_refs[k][...] = total[:, k * n : (k + 1) * n].astype(BF16)

    own_back, *back_parts = call(
        back_second,
        [sds((width, n), F32)] + [sds((width, n), BF16)] * (grid_rows - 1),
        [cell, back_a, own_grad, *far],
        "back_second",
        cost=work,
    )
    back_in = [swap(part, "row", k + 1) for k, part in enumerate(back_parts)]

    def finish(own_ref, *refs):
        *in_refs, out_ref = refs
        total = own_ref[...]
        for ref in in_refs:
            total = total + ref[...].astype(F32)
        out_ref[...] = total.T.astype(BF16)

    feat_grad = call(finish, sds((n, width), BF16), [own_back, *back_in], "finish")

    def join(place_ref, mine_ref, other_ref, out_ref):
        x = place_ref[0] & 1
        out_ref[pl.ds(pl.multiple_of(x * piece, piece), piece), :] = mine_ref[:piece]
        out_ref[pl.ds(pl.multiple_of((1 - x) * piece, piece), piece), :] = other_ref[:piece]

    g_half = call(join, sds((width, width), BF16), [place, g_piece, g_other], "join", smem=1)
    g_half_in = swap(g_half, "col", 1)

    def scale(place_ref, a_ref, b_ref, line_ref, self_ref, neigh_ref, bias_ref):
        first = (place_ref[1] & 1) == 0
        a, b = a_ref[...].astype(F32), b_ref[...].astype(F32)
        self_ref[...] = jnp.where(first, a, b) * grad_scale
        neigh_ref[...] = jnp.where(first, b, a) * grad_scale
        bias_ref[...] = line_ref[piece : piece + 1].astype(F32) * grad_scale

    grad_self, grad_neigh, grad_bias = call(
        scale,
        [sds((width, width), F32), sds((width, width), F32), sds((1, width), F32)],
        [place, g_half, g_half_in, g_piece],
        "scale",
        smem=1,
    )
    return hidden, feat_grad, grad_self, grad_neigh, grad_bias.reshape(width)


def on_device(*args):
    node_feats, tiles = args[0], args[5]
    n, width = node_feats.shape
    grid_rows, grid_cols = lax.axis_size("row"), lax.axis_size("col")
    powers = all(s & (s - 1) == 0 and s >= 2 for s in (grid_rows, grid_cols))
    dense_cell = grid_rows * grid_cols <= tiles.shape[2]
    if powers and dense_cell and n == tiles.shape[-1] and n == 128 and width % 256 == 0:
        return direct_form(*args)
    return general_form(*args)


def solution(mesh):
    placed = (
        P(("row", "col"), None),
        P(("row", "col")),
        P(),
        P(),
        P(),
        P("row", "col", None, None, None),
        P("row", "col", None),
        P("row", "col", None),
        P("row", "col"),
        P(("row", "col"), None),
    )
    return jax.shard_map(
        on_device,
        mesh=mesh,
        in_specs=placed,
        out_specs=(P(("row", "col"), None), P(("row", "col"), None), P(), P(), P()),
        check_vma=False,
    )
```

```python
import functools
import math

import jax
import jax.numpy as jnp
from jax import lax
from jax.experimental import pallas as pl
from jax.experimental.pallas import tpu as pltpu
from jax.sharding import PartitionSpec as P

F32 = jnp.float32
BF16 = jnp.bfloat16
LAST = (((1,), (1,)), ((), ()))
FIRST = (((0,), (0,)), ((), ()))


def tile_products(block_vals, near_index, far_index, live_count, source, out_blocks, transposed):
    tile_total = block_vals.shape[0]
    group_size = min(16, tile_total)
    tile_edge = block_vals.shape[-1]
    feat_width = source.shape[-1]
    source_blocks = source.reshape(source.shape[0] // tile_edge, tile_edge, feat_width)
    turn_count = (live_count + group_size - 1) // group_size

    def advance(turn, running):
        first_tile = turn * group_size
        group_vals = lax.dynamic_slice_in_dim(block_vals, first_tile, group_size, 0)
        fetch_index = lax.dynamic_slice_in_dim(far_index, first_tile, group_size, 0)
        place_index = lax.dynamic_slice_in_dim(near_index, first_tile, group_size, 0)
        picked = source_blocks[fetch_index]
        if transposed:
            products = jnp.einsum("kab,kaf->kbf", group_vals, picked, preferred_element_type=F32)
        else:
            products = jnp.einsum("kab,kbf->kaf", group_vals, picked, preferred_element_type=F32)
        ordinal = first_tile + jnp.arange(group_size)
        active = ordinal < live_count
        table = (
            (place_index[:, None] == jnp.arange(out_blocks)[None, :]) & active[:, None]
        ).astype(F32)
        return running + jnp.einsum("kl,kaf->laf", table, products)

    initial = jnp.zeros((out_blocks, tile_edge, feat_width), F32)
    result = lax.fori_loop(0, turn_count, advance, initial)
    return result.reshape(out_blocks * tile_edge, feat_width)


def general_form(
    node_feats,
    degrees,
    self_weight,
    neigh_weight,
    bias,
    tiles,
    tile_rows,
    tile_cols,
    tile_counts,
    out_grad,
):
    grid_rows = lax.axis_size("row")
    grid_cols = lax.axis_size("col")
    per_device = node_feats.shape[0]
    tile_edge = tiles.shape[-1]
    block_vals = tiles[0, 0]
    block_rows = tile_rows[0, 0]
    block_cols = tile_cols[0, 0]
    live_count = tile_counts[0, 0]
    row_blocks = grid_cols * per_device // tile_edge
    col_blocks = grid_rows * per_device // tile_edge
    stripe = lax.all_gather(node_feats, "row", axis=0, tiled=True)
    partial_value = tile_products(
        block_vals, block_rows, block_cols, live_count, stripe, row_blocks, False
    )
    summed = lax.psum_scatter(
        partial_value.astype(BF16), "col", scatter_dimension=0, tiled=True
    ).astype(F32)
    degree_col = degrees.astype(F32)[:, None]
    aggregate = (summed / degree_col).astype(BF16)
    preact = (
        jnp.dot(node_feats, self_weight, preferred_element_type=F32)
        + jnp.dot(aggregate, neigh_weight, preferred_element_type=F32)
        + bias
    )
    hidden = jax.nn.silu(preact).astype(BF16)
    sigmoid_val = jax.nn.sigmoid(preact)
    dpre = out_grad.astype(F32) * sigmoid_val * (1.0 + preact * (1.0 - sigmoid_val))
    dpre_b = dpre.astype(BF16)
    self_term = lax.dot_general(node_feats, dpre_b, FIRST, preferred_element_type=F32)
    neigh_term = lax.dot_general(aggregate, dpre_b, FIRST, preferred_element_type=F32)
    bias_term = jnp.sum(dpre, axis=0)
    self_total, neigh_total, bias_total = lax.psum(
        (self_term, neigh_term, bias_term), ("row", "col")
    )
    grad_scale = 1.0 / math.sqrt(grid_rows * grid_cols * per_device)
    back_agg = lax.dot_general(dpre_b, neigh_weight, LAST, preferred_element_type=F32)
    spread = (back_agg / degree_col).astype(BF16)
    row_stripe = lax.all_gather(spread, "col", axis=0, tiled=True)
    back_partial = tile_products(
        block_vals, block_cols, block_rows, live_count, row_stripe, col_blocks, True
    )
    neighbour_grad = lax.psum_scatter(
        back_partial.astype(BF16), "row", scatter_dimension=0, tiled=True
    ).astype(F32)
    own_grad = lax.dot_general(dpre_b, self_weight, LAST, preferred_element_type=F32)
    feat_grad = (own_grad + neighbour_grad).astype(BF16)
    return (
        hidden,
        feat_grad,
        self_total * grad_scale,
        neigh_total * grad_scale,
        bias_total * grad_scale,
    )


def sds(shape, dtype):
    return jax.ShapeDtypeStruct(shape, dtype)


def call(kernel, outs, args, name, smem=0, after=(), cost=None):
    single = not isinstance(outs, (list, tuple))
    outs = [outs] if single else list(outs)
    count = len(args)
    in_specs = [pl.BlockSpec(memory_space=pltpu.SMEM)] * smem
    in_specs += [pl.BlockSpec(memory_space=pltpu.VMEM)] * (count - smem)
    in_specs += [pl.BlockSpec(memory_space=pl.ANY)] * len(after)

    def body(*refs):
        kernel(*refs[:count], *refs[count + len(after) :])

    flops, moved = cost or (1 << 20, 1 << 18)
    result = pl.pallas_call(
        body,
        out_shape=outs,
        in_specs=in_specs,
        out_specs=[pl.BlockSpec(memory_space=pltpu.VMEM)] * len(outs),
        compiler_params=pltpu.CompilerParams(vmem_limit_bytes=24 << 20),
        cost_estimate=pl.CostEstimate(flops=flops, bytes_accessed=moved, transcendentals=0),
        name=name,
    )(*args, *after)
    return result[0] if single else result


def dot(a, b):
    return jnp.dot(a, b, preferred_element_type=F32)


def build_cell(place, tile_counts, tile_rows, tile_cols, tiles, grid_rows, grid_cols):
    total, edge = tiles.shape[0], tiles.shape[-1]
    group = 16 if total % 16 == 0 else total
    groups = total // group
    half = grid_cols // 2

    def body(place_ref, *refs):
        count_ref, rows_hbm, cols_hbm, tiles_hbm, cell_ref = refs[:5]
        sums, vals, rows, cols, sems = refs[5:]
        copies = [
            pltpu.make_async_copy(rows_hbm, rows, sems.at[groups]),
            pltpu.make_async_copy(cols_hbm, cols, sems.at[groups + 1]),
        ]
        for g in range(groups):
            span = pl.ds(g * group, group)
            copies.append(pltpu.make_async_copy(tiles_hbm.at[span], vals.at[span], sems.at[g]))
        for copy in copies:
            copy.start()
        sums[...] = jnp.zeros_like(sums)
        my_row, my_col = place_ref[0], place_ref[1]

        def add_tile(k, carry):
            near = rows[k] ^ my_col
            far = cols[k] ^ my_row
            slot = ((near >> 1) + half * (near & 1)) * grid_rows + far
            sums[slot] += vals[k].astype(F32)
            return carry

        copies[0].wait()
        copies[1].wait()
        count = count_ref[0, 0]
        for g in range(groups):
            copies[2 + g].wait()
            lax.fori_loop(g * group, jnp.clip(count, g * group, (g + 1) * group), add_tile, 0)
        for i in range(grid_cols):
            for j in range(grid_rows):
                cell_ref[i * edge : (i + 1) * edge, j * edge : (j + 1) * edge] = sums[
                    i * grid_rows + j
                ].astype(BF16)

    held = pl.BlockSpec(memory_space=pltpu.HBM)
    stored = [
        pltpu.with_memory_space_constraint(v, pltpu.HBM)
        for v in (tile_rows, tile_cols, tiles)
    ]
    return pl.pallas_call(
        body,
        out_shape=sds((grid_cols * edge, grid_rows * edge), BF16),
        in_specs=[pl.BlockSpec(memory_space=pltpu.SMEM)] * 2 + [held] * 3,
        out_specs=pl.BlockSpec(memory_space=pltpu.VMEM),
        scratch_shapes=[
            pltpu.VMEM((grid_rows * grid_cols, edge, edge), F32),
            pltpu.VMEM((total, edge, edge), BF16),
            pltpu.SMEM((total,), jnp.int32),
            pltpu.SMEM((total,), jnp.int32),
            pltpu.SemaphoreType.DMA((groups + 2,)),
        ],
        compiler_params=pltpu.CompilerParams(vmem_limit_bytes=24 << 20),
        cost_estimate=pl.CostEstimate(
            flops=1 << 24, bytes_accessed=4 * total * edge * edge, transcendentals=0
        ),
        name="build_cell",
    )(place, tile_counts, *stored)


def swap(value, axis, distance):
    size = lax.axis_size(axis)
    return lax.ppermute(value, axis, [(i, i ^ distance) for i in range(size)])


def swap_corner(value):
    size = lax.axis_size("row") * lax.axis_size("col")
    step = lax.axis_size("col") + 1
    return lax.ppermute(value, ("row", "col"), [(i, i ^ step) for i in range(size)])


def direct_form(
    node_feats,
    degrees,
    self_weight,
    neigh_weight,
    bias,
    tiles,
    tile_rows,
    tile_cols,
    tile_counts,
    out_grad,
):
    grid_rows = lax.axis_size("row")
    grid_cols = lax.axis_size("col")
    half = grid_cols // 2
    n, width = node_feats.shape
    grad_scale = 1.0 / math.sqrt(grid_rows * grid_cols * n)
    place = jnp.stack([lax.axis_index("row"), lax.axis_index("col")])

    feats = [node_feats] + [swap(node_feats, "row", k) for k in range(1, grid_rows)]

    cell = build_cell(
        place, tile_counts, tile_rows[0, 0], tile_cols[0, 0], tiles[0, 0], grid_rows, grid_cols
    )

    def prepare(x_ref, w_ref, b_ref, d_ref, pre_ref, deg_ref, degrow_ref):
        pre_ref[...] = dot(x_ref[...], w_ref[...]) + b_ref[...]
        line = d_ref[...].astype(F32)
        degrow_ref[...] = line
        deg_ref[...] = jnp.broadcast_to(line, (n, n)).T

    pre, deg, deg_row = call(
        prepare,
        [sds((n, width), F32), sds((n, n), F32), sds((1, n), F32)],
        [node_feats, self_weight, bias.reshape(1, width), degrees.reshape(1, n)],
        "prepare",
    )

    def products(part, cell_ref, *refs):
        *x_refs, out_ref = refs
        stripe = jnp.concatenate([r[...] for r in x_refs], axis=0)
        rows = half * n
        out_ref[...] = dot(cell_ref[part * rows : (part + 1) * rows, :], stripe).astype(
            out_ref.dtype
        )

    work = (2 * half * n * grid_rows * n * width, 1 << 20)
    sent = call(
        functools.partial(products, 1),
        sds((half * n, width), BF16),
        [cell, *feats],
        "forward_sent",
        cost=work,
    )
    sent_in = swap(sent, "col", 1)
    kept = call(
        functools.partial(products, 0),
        sds((half * n, width), F32),
        [cell, *feats],
        "forward_kept",
        cost=work,
    )

    def pair_sums(kept_ref, in_ref, own_ref, *out_refs):
        total = kept_ref[...] + in_ref[...].astype(F32)
        own_ref[...] = total[:n]
        for q, ref in enumerate(out_refs):
            ref[...] = total[(q + 1) * n : (q + 2) * n].astype(BF16)

    own_sum, *parts = call(
        pair_sums,
        [sds((n, width), F32)] + [sds((n, width), BF16)] * (half - 1),
        [kept, sent_in],
        "pair_sums",
    )
    parts_in = [swap(part, "col", 2 * (q + 1)) for q, part in enumerate(parts)]

    pad = 16
    piece = width // 2
    small = sds((piece + pad, width), BF16)
    inward = half - 1

    def dense(place_ref, own_ref, *refs):
        in_refs, refs = refs[:inward], refs[inward:]
        x_ref, pre_ref, deg_ref, degrow_ref, ws_ref, wn_ref, g_ref = refs[:7]
        spread_ref, preact_ref, back_ref, *out_refs = refs[7:]
        total = own_ref[...]
        for ref in in_refs:
            total = total + ref[...].astype(F32)
        d = deg_ref[...]
        agg = (total / jnp.concatenate([d] * (width // n), axis=1)).astype(BF16)
        v = pre_ref[...] + dot(agg, wn_ref[...])
        preact_ref[...] = v
        s = jax.nn.sigmoid(v)
        dpre = g_ref[...].astype(F32) * s * (1.0 + v * (1.0 - s))
        dpre_b = dpre.astype(BF16)
        line = jnp.broadcast_to(jnp.sum(dpre, axis=0, keepdims=True), (pad, width)).astype(BF16)
        on_first = (place_ref[1] & 1) == 0
        on_left = (place_ref[0] & 1) == 0
        feats_own = x_ref[...]
        mine = jnp.where(on_first, feats_own, agg)
        other = jnp.where(on_first, agg, feats_own)
        for ref, source, left in (
            (out_refs[1], other, on_left),
            (out_refs[2], mine, ~on_left),
            (out_refs[3], other, ~on_left),
            (out_refs[0], mine, on_left),
        ):
            block = jnp.where(left, source[:, :piece], source[:, piece:])
            ref[:piece] = lax.dot_general(
                block, dpre_b, FIRST, preferred_element_type=F32
            ).astype(BF16)
            ref[piece:] = line
        back = lax.dot_general(wn_ref[...], dpre_b, LAST, preferred_element_type=F32)
        spread_ref[...] = (back / degrow_ref[...]).astype(BF16)
        back_ref[...] = lax.dot_general(ws_ref[...], dpre_b, LAST, preferred_element_type=F32)

    spread, preact, own_grad, g_own, g_core, g_side, g_corner = call(
        dense,
        [sds((width, n), BF16), sds((n, width), F32), sds((width, n), F32)] + [small] * 4,
        [
            place,
            own_sum,
            *parts_in[::-1],
            node_feats,
            pre,
            deg,
            deg_row,
            self_weight,
            neigh_weight,
            out_grad,
        ],
        "dense",
        smem=1,
    )
    near = [spread] + [swap(spread, "col", 2 * q) for q in range(1, half)]

    def add_many(*refs):
        *in_refs, out_ref = refs
        vals = [ref[...].astype(F32) for ref in in_refs]
        while len(vals) > 1:
            vals = [vals[i] + vals[i + 1] for i in range(0, len(vals), 2)]
        out_ref[...] = vals[0].astype(BF16)

    g_in = [swap_corner(g_corner), swap(g_side, "row", 1), swap(g_core, "col", 1)]
    g_part = call(add_many, small, [g_own, *g_in[::-1]], "add_corner", after=())
    y_in = [swap(g_part, "row", 2 ** i) for i in range(1, grid_rows.bit_length() - 1)]

    far = [swap(part, "col", 1) for part in near]

    def back_first(cell_ref, *refs):
        *s_refs, out_ref = refs
        left = jnp.concatenate([r[...] for r in s_refs], axis=1)
        out_ref[...] = dot(left, cell_ref[: half * n, :])

    back_a = call(
        back_first, sds((width, grid_rows * n), F32), [cell, *near], "back_first", cost=work
    )

    def back_second(cell_ref, a_ref, base_ref, *refs):
        s_refs, out_refs = refs[:half], refs[half:]
        left = jnp.concatenate([r[...] for r in s_refs], axis=1)
        total = a_ref[...] + dot(left, cell_ref[half * n :, :])
        out_refs[0][...] = total[:, :n] + base_ref[...]
        for k in range(1, grid_rows):
            out_refs[k][...] = total[:, k * n : (k + 1) * n].astype(BF16)

    own_back, *back_parts = call(
        back_second,
        [sds((width, n), F32)] + [sds((width, n), BF16)] * (grid_rows - 1),
        [cell, back_a, own_grad, *far],
        "back_second",
        cost=work,
    )
    back_in = [swap(part, "row", k + 1) for k, part in enumerate(back_parts)]

    def activate(v_ref, hid_ref):
        v = v_ref[...]
        hid_ref[...] = (v * jax.nn.sigmoid(v)).astype(BF16)

    hidden = call(activate, sds((n, width), BF16), [preact], "activate", after=[own_back])

    def finish(own_ref, *refs):
        *in_refs, out_ref = refs
        total = own_ref[...]
        for ref in in_refs:
            total = total + ref[...].astype(F32)
        out_ref[...] = total.T.astype(BF16)

    feat_grad = call(finish, sds((n, width), BF16), [own_back, *back_in], "finish")

    z_part = g_part
    for got in y_in:
        z_part = call(add_many, small, [z_part, got], "add_y", after=near[1:])
    z_in = [swap(z_part, "col", 2 * q) for q in range(1, half)]
    g_piece = call(add_many, small, [z_part, *z_in], "add_z", after=[own_back])
    pieces = g_piece[:piece]
    pieces_in = [swap_corner(pieces), swap(pieces, "row", 1), swap(pieces, "col", 1)]

    def write(flip, place_ref, a_ref, b_ref, self_hbm, neigh_hbm, blocks, sems):
        first = (place_ref[1] & 1) == 0
        row = (place_ref[0] & 1) ^ flip
        span = pl.ds(pl.multiple_of(row * piece, piece), piece)
        a = a_ref[:piece].astype(F32) * grad_scale
        b = b_ref[:piece].astype(F32) * grad_scale
        copies = []
        for j, (value, out) in enumerate(
            ((jnp.where(first, a, b), self_hbm), (jnp.where(first, b, a), neigh_hbm))
        ):
            blocks[j] = value
            copies.append(pltpu.make_async_copy(blocks.at[j], out.at[span], sems.at[j]))
            copies[-1].start()
        for copy in copies:
            copy.wait()

    def write_first(place_ref, a_ref, b_ref, self_hbm, neigh_hbm, bias_ref, blocks, sems):
        bias_ref[...] = a_ref[piece : piece + 1].astype(F32) * grad_scale
        write(0, place_ref, a_ref, b_ref, self_hbm, neigh_hbm, blocks, sems)

    def write_second(place_ref, a_ref, b_ref, s_ref, n_ref, self_hbm, neigh_hbm, blocks, sems):
        write(1, place_ref, a_ref, b_ref, self_hbm, neigh_hbm, blocks, sems)

    held, fast = (pl.BlockSpec(memory_space=m) for m in (pltpu.HBM, pltpu.VMEM))
    whole = [sds((width, width), F32)] * 2
    common = dict(
        scratch_shapes=[pltpu.VMEM((2, piece, width), F32), pltpu.SemaphoreType.DMA((2,))],
        compiler_params=pltpu.CompilerParams(vmem_limit_bytes=24 << 20),
        cost_estimate=pl.CostEstimate(flops=1 << 20, bytes_accessed=1 << 18, transcendentals=0),
    )
    scalars = pl.BlockSpec(memory_space=pltpu.SMEM)
    corner_in, side_in, core_in = pieces_in
    *grads, grad_bias = pl.pallas_call(
        write_first,
        out_shape=whole + [sds((1, width), F32)],
        in_specs=[scalars, fast, fast],
        out_specs=[held, held, fast],
        name="write_first",
        **common,
    )(place, g_piece, core_in)
    grad_self, grad_neigh = pl.pallas_call(
        write_second,
        out_shape=whole,
        in_specs=[scalars, fast, fast, held, held],
        out_specs=[held, held],
        input_output_aliases={3: 0, 4: 1},
        name="write_second",
        **common,
    )(place, side_in, corner_in, *grads)
    return hidden, feat_grad, grad_self, grad_neigh, grad_bias.reshape(width)


def on_device(*args):
    node_feats, tiles = args[0], args[5]
    n, width = node_feats.shape
    grid_rows, grid_cols = lax.axis_size("row"), lax.axis_size("col")
    powers = all(s & (s - 1) == 0 and s >= 2 for s in (grid_rows, grid_cols))
    dense_cell = grid_rows * grid_cols <= tiles.shape[2]
    if powers and dense_cell and n == tiles.shape[-1] and n == 128 and width % 256 == 0:
        return direct_form(*args)
    return general_form(*args)


def solution(mesh):
    placed = (
        P(("row", "col"), None),
        P(("row", "col")),
        P(),
        P(),
        P(),
        P("row", "col", None, None, None),
        P("row", "col", None),
        P("row", "col", None),
        P("row", "col"),
        P(("row", "col"), None),
    )
    return jax.shard_map(
        on_device,
        mesh=mesh,
        in_specs=placed,
        out_specs=(P(("row", "col"), None), P(("row", "col"), None), P(), P(), P()),
        check_vma=False,
    )
```

```python
import functools
import math

import jax
import jax.numpy as jnp
from jax import lax
from jax.experimental import pallas as pl
from jax.experimental.pallas import tpu as pltpu
from jax.sharding import PartitionSpec as P

F32 = jnp.float32
BF16 = jnp.bfloat16
STRIP = 16
LAST = (((1,), (1,)), ((), ()))
FIRST = (((0,), (0,)), ((), ()))


def tile_products(block_vals, near_index, far_index, live_count, source, out_blocks, transposed):
    tile_total = block_vals.shape[0]
    group_size = min(16, tile_total)
    tile_edge = block_vals.shape[-1]
    feat_width = source.shape[-1]
    source_blocks = source.reshape(source.shape[0] // tile_edge, tile_edge, feat_width)
    turn_count = (live_count + group_size - 1) // group_size

    def advance(turn, running):
        first_tile = turn * group_size
        group_vals = lax.dynamic_slice_in_dim(block_vals, first_tile, group_size, 0)
        fetch_index = lax.dynamic_slice_in_dim(far_index, first_tile, group_size, 0)
        place_index = lax.dynamic_slice_in_dim(near_index, first_tile, group_size, 0)
        picked = source_blocks[fetch_index]
        if transposed:
            products = jnp.einsum("kab,kaf->kbf", group_vals, picked, preferred_element_type=F32)
        else:
            products = jnp.einsum("kab,kbf->kaf", group_vals, picked, preferred_element_type=F32)
        ordinal = first_tile + jnp.arange(group_size)
        active = ordinal < live_count
        table = (
            (place_index[:, None] == jnp.arange(out_blocks)[None, :]) & active[:, None]
        ).astype(F32)
        return running + jnp.einsum("kl,kaf->laf", table, products)

    initial = jnp.zeros((out_blocks, tile_edge, feat_width), F32)
    result = lax.fori_loop(0, turn_count, advance, initial)
    return result.reshape(out_blocks * tile_edge, feat_width)


def general_form(
    node_feats,
    degrees,
    self_weight,
    neigh_weight,
    bias,
    tiles,
    tile_rows,
    tile_cols,
    tile_counts,
    out_grad,
):
    grid_rows = lax.axis_size("row")
    grid_cols = lax.axis_size("col")
    per_device = node_feats.shape[0]
    tile_edge = tiles.shape[-1]
    block_vals = tiles[0, 0]
    block_rows = tile_rows[0, 0]
    block_cols = tile_cols[0, 0]
    live_count = tile_counts[0, 0]
    row_blocks = grid_cols * per_device // tile_edge
    col_blocks = grid_rows * per_device // tile_edge
    stripe = lax.all_gather(node_feats, "row", axis=0, tiled=True)
    partial_value = tile_products(
        block_vals, block_rows, block_cols, live_count, stripe, row_blocks, False
    )
    summed = lax.psum_scatter(
        partial_value.astype(BF16), "col", scatter_dimension=0, tiled=True
    ).astype(F32)
    degree_col = degrees.astype(F32)[:, None]
    aggregate = (summed / degree_col).astype(BF16)
    preact = (
        jnp.dot(node_feats, self_weight, preferred_element_type=F32)
        + jnp.dot(aggregate, neigh_weight, preferred_element_type=F32)
        + bias
    )
    hidden = jax.nn.silu(preact).astype(BF16)
    sigmoid_val = jax.nn.sigmoid(preact)
    dpre = out_grad.astype(F32) * sigmoid_val * (1.0 + preact * (1.0 - sigmoid_val))
    dpre_b = dpre.astype(BF16)
    self_term = lax.dot_general(node_feats, dpre_b, FIRST, preferred_element_type=F32)
    neigh_term = lax.dot_general(aggregate, dpre_b, FIRST, preferred_element_type=F32)
    bias_term = jnp.sum(dpre, axis=0)
    self_total, neigh_total, bias_total = lax.psum(
        (self_term, neigh_term, bias_term), ("row", "col")
    )
    grad_scale = 1.0 / math.sqrt(grid_rows * grid_cols * per_device)
    back_agg = lax.dot_general(dpre_b, neigh_weight, LAST, preferred_element_type=F32)
    spread = (back_agg / degree_col).astype(BF16)
    row_stripe = lax.all_gather(spread, "col", axis=0, tiled=True)
    back_partial = tile_products(
        block_vals, block_cols, block_rows, live_count, row_stripe, col_blocks, True
    )
    neighbour_grad = lax.psum_scatter(
        back_partial.astype(BF16), "row", scatter_dimension=0, tiled=True
    ).astype(F32)
    own_grad = lax.dot_general(dpre_b, self_weight, LAST, preferred_element_type=F32)
    feat_grad = (own_grad + neighbour_grad).astype(BF16)
    return (
        hidden,
        feat_grad,
        self_total * grad_scale,
        neigh_total * grad_scale,
        bias_total * grad_scale,
    )


def sds(shape, dtype):
    return jax.ShapeDtypeStruct(shape, dtype)


def call(kernel, outs, args, name, after=(), cost=None):
    single = not isinstance(outs, (list, tuple))
    outs = [outs] if single else list(outs)
    count = len(args)
    in_specs = [pl.BlockSpec(memory_space=pltpu.VMEM)] * count
    in_specs += [pl.BlockSpec(memory_space=pl.ANY)] * len(after)

    def body(*refs):
        kernel(*refs[:count], *refs[count + len(after) :])

    flops, moved = cost or (1 << 20, 1 << 18)
    result = pl.pallas_call(
        body,
        out_shape=outs,
        in_specs=in_specs,
        out_specs=[pl.BlockSpec(memory_space=pltpu.VMEM)] * len(outs),
        compiler_params=pltpu.CompilerParams(vmem_limit_bytes=24 << 20),
        cost_estimate=pl.CostEstimate(flops=flops, bytes_accessed=moved, transcendentals=0),
        name=name,
    )(*args, *after)
    return result[0] if single else result


def dot(a, b):
    return jnp.dot(a, b, preferred_element_type=F32)


def build_cell(tile_counts, tile_rows, tile_cols, tiles, grid_rows, grid_cols):
    total, edge = tiles.shape[0], tiles.shape[-1]
    group = 16 if total % 16 == 0 else total
    groups = total // group
    half = grid_cols // 2

    def body(*refs):
        count_ref, rows_hbm, cols_hbm, tiles_hbm, cell_ref = refs[:5]
        sums, vals, rows, cols, sems = refs[5:]
        copies = [
            pltpu.make_async_copy(rows_hbm, rows, sems.at[groups]),
            pltpu.make_async_copy(cols_hbm, cols, sems.at[groups + 1]),
        ]
        for g in range(groups):
            span = pl.ds(g * group, group)
            copies.append(pltpu.make_async_copy(tiles_hbm.at[span], vals.at[span], sems.at[g]))
        for copy in copies:
            copy.start()
        sums[...] = jnp.zeros_like(sums)
        my_row, my_col = lax.axis_index("row"), lax.axis_index("col")

        def add_tile(k, carry):
            near = rows[k] ^ my_col
            far = cols[k] ^ my_row
            slot = ((near >> 1) + half * (near & 1)) * grid_rows + far
            sums[slot] += vals[k].astype(F32)
            return carry

        copies[0].wait()
        copies[1].wait()
        count = count_ref[0, 0]
        for g in range(groups):
            copies[2 + g].wait()
            lax.fori_loop(g * group, jnp.clip(count, g * group, (g + 1) * group), add_tile, 0)
        for i in range(grid_cols):
            for j in range(grid_rows):
                cell_ref[i * edge : (i + 1) * edge, j * edge : (j + 1) * edge] = sums[
                    i * grid_rows + j
                ].astype(BF16)

    held = pl.BlockSpec(memory_space=pltpu.HBM)
    stored = [
        pltpu.with_memory_space_constraint(v, pltpu.HBM)
        for v in (tile_rows, tile_cols, tiles)
    ]
    return pl.pallas_call(
        body,
        out_shape=sds((grid_cols * edge, grid_rows * edge), BF16),
        in_specs=[pl.BlockSpec(memory_space=pltpu.SMEM)] + [held] * 3,
        out_specs=pl.BlockSpec(memory_space=pltpu.VMEM),
        scratch_shapes=[
            pltpu.VMEM((grid_rows * grid_cols, edge, edge), F32),
            pltpu.VMEM((total, edge, edge), BF16),
            pltpu.SMEM((total,), jnp.int32),
            pltpu.SMEM((total,), jnp.int32),
            pltpu.SemaphoreType.DMA((groups + 2,)),
        ],
        compiler_params=pltpu.CompilerParams(vmem_limit_bytes=24 << 20),
        cost_estimate=pl.CostEstimate(
            flops=1 << 24, bytes_accessed=4 * total * edge * edge, transcendentals=0
        ),
        name="build_cell",
    )(tile_counts, *stored)


def swap(value, axis, distance):
    size = lax.axis_size(axis)
    return lax.ppermute(value, axis, [(i, i ^ distance) for i in range(size)])


def swap_corner(value):
    size = lax.axis_size("row") * lax.axis_size("col")
    step = lax.axis_size("col") + 1
    return lax.ppermute(value, ("row", "col"), [(i, i ^ step) for i in range(size)])


def direct_form(
    node_feats,
    degrees,
    self_weight,
    neigh_weight,
    bias,
    tiles,
    tile_rows,
    tile_cols,
    tile_counts,
    out_grad,
):
    grid_rows = lax.axis_size("row")
    grid_cols = lax.axis_size("col")
    half = grid_cols // 2
    n, width = node_feats.shape
    grad_scale = 1.0 / math.sqrt(grid_rows * grid_cols * n)

    feats = [node_feats] + [swap(node_feats, "row", k) for k in range(1, grid_rows)]

    cell = build_cell(
        tile_counts, tile_rows[0, 0], tile_cols[0, 0], tiles[0, 0], grid_rows, grid_cols
    )

    def prepare(x_ref, w_ref, b_ref, d_ref, pre_ref, deg_ref, degrow_ref):
        pre_ref[...] = dot(x_ref[...], w_ref[...]) + b_ref[...]
        line = d_ref[...].astype(F32)
        degrow_ref[...] = line
        deg_ref[...] = jnp.broadcast_to(line, (n, n)).T

    pre, deg, deg_row = call(
        prepare,
        [sds((n, width), F32), sds((n, n), F32), sds((1, n), F32)],
        [node_feats, self_weight, bias.reshape(1, width), degrees.reshape(1, n)],
        "prepare",
    )

    def products(part, cell_ref, *refs):
        *x_refs, out_ref = refs
        stripe = jnp.concatenate([r[...] for r in x_refs], axis=0)
        rows = half * n
        out_ref[...] = dot(cell_ref[part * rows : (part + 1) * rows, :], stripe).astype(
            out_ref.dtype
        )

    work = (2 * half * n * grid_rows * n * width, 1 << 20)
    sent = call(
        functools.partial(products, 1),
        sds((half * n, width), BF16),
        [cell, *feats],
        "forward_sent",
        cost=work,
    )
    sent_in = swap(sent, "col", 1)
    kept = call(
        functools.partial(products, 0),
        sds((half * n, width), F32),
        [cell, *feats],
        "forward_kept",
        cost=work,
    )

    def pair_sums(kept_ref, in_ref, own_ref, *out_refs):
        total = kept_ref[...] + in_ref[...].astype(F32)
        own_ref[...] = total[:n]
        for q, ref in enumerate(out_refs):
            ref[...] = total[(q + 1) * n : (q + 2) * n].astype(BF16)

    own_sum, *parts = call(
        pair_sums,
        [sds((n, width), F32)] + [sds((n, width), BF16)] * (half - 1),
        [kept, sent_in],
        "pair_sums",
    )
    parts_in = [swap(part, "col", 2 * (q + 1)) for q, part in enumerate(parts)]

    pad = 16
    piece = width // 2
    small = sds((piece + pad, width), BF16)
    inward = half - 1

    def dense(own_ref, *refs):
        in_refs, refs = refs[:inward], refs[inward:]
        x_ref, pre_ref, deg_ref, degrow_ref, wn_ref, g_ref = refs[:6]
        spread_ref, preact_ref, dpre_ref, *out_refs = refs[6:]
        total = own_ref[...]
        for ref in in_refs:
            total = total + ref[...].astype(F32)
        d = deg_ref[...]
        agg = (total / jnp.concatenate([d] * (width // n), axis=1)).astype(BF16)
        v = pre_ref[...] + dot(agg, wn_ref[...])
        preact_ref[...] = v
        s = jax.nn.sigmoid(v)
        dpre = g_ref[...].astype(F32) * s * (1.0 + v * (1.0 - s))
        dpre_b = dpre.astype(BF16)
        dpre_ref[...] = dpre_b
        line = jnp.broadcast_to(jnp.sum(dpre, axis=0, keepdims=True), (pad, width)).astype(BF16)
        on_first = (lax.axis_index("col") & 1) == 0
        on_left = (lax.axis_index("row") & 1) == 0
        feats_own = x_ref[...]
        mine = jnp.where(on_first, feats_own, agg)
        other = jnp.where(on_first, agg, feats_own)
        for ref, source, left in (
            (out_refs[1], other, on_left),
            (out_refs[2], mine, ~on_left),
            (out_refs[3], other, ~on_left),
            (out_refs[0], mine, on_left),
        ):
            block = jnp.where(left, source[:, :piece], source[:, piece:])
            ref[:piece] = lax.dot_general(
                block, dpre_b, FIRST, preferred_element_type=F32
            ).astype(BF16)
            ref[piece:] = line
        back = lax.dot_general(wn_ref[...], dpre_b, LAST, preferred_element_type=F32)
        spread_ref[...] = (back / degrow_ref[...]).astype(BF16)

    spread, preact, dpre_b, g_own, g_core, g_side, g_corner = call(
        dense,
        [sds((width, n), BF16), sds((n, width), F32), sds((n, width), BF16)] + [small] * 4,
        [
            own_sum,
            *parts_in[::-1],
            node_feats,
            pre,
            deg,
            deg_row,
            neigh_weight,
            out_grad,
        ],
        "dense",
    )
    near = [spread] + [swap(spread, "col", 2 * q) for q in range(1, half)]

    def add_many(*refs):
        *in_refs, out_ref = refs
        vals = [ref[...].astype(F32) for ref in in_refs]
        while len(vals) > 1:
            vals = [vals[i] + vals[i + 1] for i in range(0, len(vals), 2)]
        out_ref[...] = vals[0].astype(BF16)

    g_in = [swap_corner(g_corner), swap(g_side, "row", 1), swap(g_core, "col", 1)]
    g_part = call(add_many, small, [g_own, *g_in[::-1]], "add_corner", after=())
    y_in = [swap(g_part, "row", 2 ** i) for i in range(1, grid_rows.bit_length() - 1)]

    far = [swap(part, "col", 1) for part in near]

    def back_first(cell_ref, *refs):
        *s_refs, out_ref = refs
        left = jnp.concatenate([r[...] for r in s_refs], axis=1)
        out_ref[...] = dot(left, cell_ref[: half * n, :])

    back_a = call(
        back_first, sds((width, grid_rows * n), F32), [cell, *near], "back_first", cost=work
    )

    def back_second(cell_ref, a_ref, *refs):
        s_refs, out_refs = refs[:half], refs[half:]
        left = jnp.concatenate([r[...] for r in s_refs], axis=1)
        total = a_ref[...] + dot(left, cell_ref[half * n :, :])
        out_refs[0][...] = total[:, :n]
        for k in range(1, grid_rows):
            out_refs[k][...] = total[:, k * n : (k + 1) * n].astype(BF16)

    own_back, *back_parts = call(
        back_second,
        [sds((width, n), F32)] + [sds((width, n), BF16)] * (grid_rows - 1),
        [cell, back_a, *far],
        "back_second",
        cost=work,
    )
    back_in = [swap(part, "row", k + 1) for k, part in enumerate(back_parts)]

    def activate(v_ref, w_ref, d_ref, hid_ref, own_ref):
        v = v_ref[...]
        hid_ref[...] = (v * jax.nn.sigmoid(v)).astype(BF16)
        own_ref[...] = lax.dot_general(w_ref[...], d_ref[...], LAST, preferred_element_type=F32)

    hidden, own_grad = call(
        activate,
        [sds((n, width), BF16), sds((width, n), F32)],
        [preact, self_weight, dpre_b],
        "activate",
        after=[own_back],
    )

    def finish(grad_ref, own_ref, *refs):
        *in_refs, out_ref = refs
        total = grad_ref[...] + own_ref[...]
        for ref in in_refs:
            total = total + ref[...].astype(F32)
        out_ref[...] = total.T.astype(BF16)

    feat_grad = call(finish, sds((n, width), BF16), [own_grad, own_back, *back_in], "finish")

    z_part = g_part
    for got in y_in:
        z_part = call(add_many, small, [z_part, got], "add_y", after=near[1:])
    z_in = [swap(z_part, "col", 2 * q) for q in range(1, half)]
    g_piece = call(add_many, small, [z_part, *z_in], "add_z", after=[own_back])
    pieces = g_piece[:piece]
    pieces_in = [swap_corner(pieces), swap(pieces, "row", 1), swap(pieces, "col", 1)]

    def write(parts, hbms, blocks, sems):
        x, c = lax.axis_index("row") & 1, lax.axis_index("col") & 1
        for j, (ref, side, core) in enumerate(parts):
            blocks[j] = ref[:piece].astype(F32) * grad_scale
            base = (x ^ side) * piece
            for which, hbm in enumerate(hbms):

                @pl.when((c ^ core) == which)
                def _():
                    for i in range(0, piece, STRIP):
                        to = pl.ds(pl.multiple_of(base + i, STRIP), STRIP)
                        pltpu.make_async_copy(
                            blocks.at[j, pl.ds(i, STRIP)], hbm.at[to], sems.at[j]
                        ).start()

    def drain(count, hbm, blocks, sems):
        for j in range(count):
            pltpu.make_async_copy(blocks.at[j], hbm.at[pl.ds(0, piece)], sems.at[j]).wait()

    def write_first(a_ref, b_ref, self_hbm, neigh_hbm, bias_hbm, blocks, sems, line):
        line[...] = a_ref[piece : piece + 1].astype(F32) * grad_scale
        copy = pltpu.make_async_copy(line, bias_hbm, sems.at[2])
        copy.start()
        parts = ((a_ref, 0, 0), (b_ref, 0, 1))
        write(parts, (self_hbm, neigh_hbm), blocks, sems)
        drain(2, self_hbm, blocks, sems)
        copy.wait()

    def write_next(core, a_ref, s_ref, n_ref, self_hbm, neigh_hbm, blocks, sems):
        write(((a_ref, 1, core),), (self_hbm, neigh_hbm), blocks, sems)
        drain(1, self_hbm, blocks, sems)

    held, fast = (pl.BlockSpec(memory_space=m) for m in (pltpu.HBM, pltpu.VMEM))
    whole = [sds((width, width), F32)] * 2
    common = dict(
        compiler_params=pltpu.CompilerParams(vmem_limit_bytes=24 << 20),
        cost_estimate=pl.CostEstimate(flops=1 << 20, bytes_accessed=1 << 18, transcendentals=0),
    )
    scratch = [pltpu.VMEM((2, piece, width), F32), pltpu.SemaphoreType.DMA((3,))]
    corner_in, side_in, core_in = pieces_in
    *grads, grad_bias = pl.pallas_call(
        write_first,
        out_shape=whole + [sds((1, width), F32)],
        in_specs=[fast, fast],
        out_specs=[held, held, held],
        scratch_shapes=scratch + [pltpu.VMEM((1, width), F32)],
        name="write_first",
        **common,
    )(g_piece, core_in)
    for core, got in ((1, corner_in), (0, side_in)):
        grads = pl.pallas_call(
            functools.partial(write_next, core),
            out_shape=whole,
            in_specs=[fast, held, held],
            out_specs=[held, held],
            input_output_aliases={1: 0, 2: 1},
            scratch_shapes=scratch,
            name="write_next",
            **common,
        )(got, *grads)
    grad_self, grad_neigh = grads
    return hidden, feat_grad, grad_self, grad_neigh, grad_bias.reshape(width)


def on_device(*args):
    node_feats, tiles = args[0], args[5]
    n, width = node_feats.shape
    grid_rows, grid_cols = lax.axis_size("row"), lax.axis_size("col")
    powers = all(s & (s - 1) == 0 and s >= 2 for s in (grid_rows, grid_cols))
    dense_cell = grid_rows * grid_cols <= tiles.shape[2]
    if powers and dense_cell and n == tiles.shape[-1] and n == 128 and width % 256 == 0:
        return direct_form(*args)
    return general_form(*args)


def solution(mesh):
    placed = (
        P(("row", "col"), None),
        P(("row", "col")),
        P(),
        P(),
        P(),
        P("row", "col", None, None, None),
        P("row", "col", None),
        P("row", "col", None),
        P("row", "col"),
        P(("row", "col"), None),
    )
    return jax.shard_map(
        on_device,
        mesh=mesh,
        in_specs=placed,
        out_specs=(P(("row", "col"), None), P(("row", "col"), None), P(), P(), P()),
        check_vma=False,
    )
```

```python
import functools
import math

import jax
import jax.numpy as jnp
from jax import lax
from jax.experimental import pallas as pl
from jax.experimental.pallas import tpu as pltpu
from jax.sharding import PartitionSpec as P

F32 = jnp.float32
BF16 = jnp.bfloat16
STRIP = 16
LAST = (((1,), (1,)), ((), ()))
FIRST = (((0,), (0,)), ((), ()))


def tile_products(block_vals, near_index, far_index, live_count, source, out_blocks, transposed):
    tile_total = block_vals.shape[0]
    group_size = min(16, tile_total)
    tile_edge = block_vals.shape[-1]
    feat_width = source.shape[-1]
    source_blocks = source.reshape(source.shape[0] // tile_edge, tile_edge, feat_width)
    turn_count = (live_count + group_size - 1) // group_size

    def advance(turn, running):
        first_tile = turn * group_size
        group_vals = lax.dynamic_slice_in_dim(block_vals, first_tile, group_size, 0)
        fetch_index = lax.dynamic_slice_in_dim(far_index, first_tile, group_size, 0)
        place_index = lax.dynamic_slice_in_dim(near_index, first_tile, group_size, 0)
        picked = source_blocks[fetch_index]
        if transposed:
            products = jnp.einsum("kab,kaf->kbf", group_vals, picked, preferred_element_type=F32)
        else:
            products = jnp.einsum("kab,kbf->kaf", group_vals, picked, preferred_element_type=F32)
        ordinal = first_tile + jnp.arange(group_size)
        active = ordinal < live_count
        table = (
            (place_index[:, None] == jnp.arange(out_blocks)[None, :]) & active[:, None]
        ).astype(F32)
        return running + jnp.einsum("kl,kaf->laf", table, products)

    initial = jnp.zeros((out_blocks, tile_edge, feat_width), F32)
    result = lax.fori_loop(0, turn_count, advance, initial)
    return result.reshape(out_blocks * tile_edge, feat_width)


def general_form(
    node_feats,
    degrees,
    self_weight,
    neigh_weight,
    bias,
    tiles,
    tile_rows,
    tile_cols,
    tile_counts,
    out_grad,
):
    grid_rows = lax.axis_size("row")
    grid_cols = lax.axis_size("col")
    per_device = node_feats.shape[0]
    tile_edge = tiles.shape[-1]
    block_vals = tiles[0, 0]
    block_rows = tile_rows[0, 0]
    block_cols = tile_cols[0, 0]
    live_count = tile_counts[0, 0]
    row_blocks = grid_cols * per_device // tile_edge
    col_blocks = grid_rows * per_device // tile_edge
    stripe = lax.all_gather(node_feats, "row", axis=0, tiled=True)
    partial_value = tile_products(
        block_vals, block_rows, block_cols, live_count, stripe, row_blocks, False
    )
    summed = lax.psum_scatter(
        partial_value.astype(BF16), "col", scatter_dimension=0, tiled=True
    ).astype(F32)
    degree_col = degrees.astype(F32)[:, None]
    aggregate = (summed / degree_col).astype(BF16)
    preact = (
        jnp.dot(node_feats, self_weight, preferred_element_type=F32)
        + jnp.dot(aggregate, neigh_weight, preferred_element_type=F32)
        + bias
    )
    hidden = jax.nn.silu(preact).astype(BF16)
    sigmoid_val = jax.nn.sigmoid(preact)
    dpre = out_grad.astype(F32) * sigmoid_val * (1.0 + preact * (1.0 - sigmoid_val))
    dpre_b = dpre.astype(BF16)
    self_term = lax.dot_general(node_feats, dpre_b, FIRST, preferred_element_type=F32)
    neigh_term = lax.dot_general(aggregate, dpre_b, FIRST, preferred_element_type=F32)
    bias_term = jnp.sum(dpre, axis=0)
    self_total, neigh_total, bias_total = lax.psum(
        (self_term, neigh_term, bias_term), ("row", "col")
    )
    grad_scale = 1.0 / math.sqrt(grid_rows * grid_cols * per_device)
    back_agg = lax.dot_general(dpre_b, neigh_weight, LAST, preferred_element_type=F32)
    spread = (back_agg / degree_col).astype(BF16)
    row_stripe = lax.all_gather(spread, "col", axis=0, tiled=True)
    back_partial = tile_products(
        block_vals, block_cols, block_rows, live_count, row_stripe, col_blocks, True
    )
    neighbour_grad = lax.psum_scatter(
        back_partial.astype(BF16), "row", scatter_dimension=0, tiled=True
    ).astype(F32)
    own_grad = lax.dot_general(dpre_b, self_weight, LAST, preferred_element_type=F32)
    feat_grad = (own_grad + neighbour_grad).astype(BF16)
    return (
        hidden,
        feat_grad,
        self_total * grad_scale,
        neigh_total * grad_scale,
        bias_total * grad_scale,
    )


def sds(shape, dtype):
    return jax.ShapeDtypeStruct(shape, dtype)


def call(kernel, outs, args, name, after=(), cost=None):
    single = not isinstance(outs, (list, tuple))
    outs = [outs] if single else list(outs)
    count = len(args)
    in_specs = [pl.BlockSpec(memory_space=pltpu.VMEM)] * count
    in_specs += [pl.BlockSpec(memory_space=pl.ANY)] * len(after)

    def body(*refs):
        kernel(*refs[:count], *refs[count + len(after) :])

    flops, moved = cost or (1 << 20, 1 << 18)
    result = pl.pallas_call(
        body,
        out_shape=outs,
        in_specs=in_specs,
        out_specs=[pl.BlockSpec(memory_space=pltpu.VMEM)] * len(outs),
        compiler_params=pltpu.CompilerParams(vmem_limit_bytes=24 << 20),
        cost_estimate=pl.CostEstimate(flops=flops, bytes_accessed=moved, transcendentals=0),
        name=name,
    )(*args, *after)
    return result[0] if single else result


def dot(a, b):
    return jnp.dot(a, b, preferred_element_type=F32)


def build_cell(tile_counts, tile_rows, tile_cols, tiles, grid_rows, grid_cols):
    total, edge = tiles.shape[0], tiles.shape[-1]
    group = 16 if total % 16 == 0 else total
    groups = total // group
    half = grid_cols // 2

    def body(*refs):
        count_ref, rows_hbm, cols_hbm, tiles_hbm, cell_ref = refs[:5]
        sums, vals, rows, cols, sems = refs[5:]
        copies = [
            pltpu.make_async_copy(rows_hbm, rows, sems.at[groups]),
            pltpu.make_async_copy(cols_hbm, cols, sems.at[groups + 1]),
        ]
        for g in range(groups):
            span = pl.ds(g * group, group)
            copies.append(pltpu.make_async_copy(tiles_hbm.at[span], vals.at[span], sems.at[g]))
        for copy in copies:
            copy.start()
        sums[...] = jnp.zeros_like(sums)
        my_row, my_col = lax.axis_index("row"), lax.axis_index("col")

        def add_tile(k, carry):
            near = rows[k] ^ my_col
            far = cols[k] ^ my_row
            slot = ((near >> 1) + half * (near & 1)) * grid_rows + far
            sums[slot] += vals[k].astype(F32)
            return carry

        copies[0].wait()
        copies[1].wait()
        count = count_ref[0, 0]
        for g in range(groups):
            copies[2 + g].wait()
            lax.fori_loop(g * group, jnp.clip(count, g * group, (g + 1) * group), add_tile, 0)
        for i in range(grid_cols):
            for j in range(grid_rows):
                cell_ref[i * edge : (i + 1) * edge, j * edge : (j + 1) * edge] = sums[
                    i * grid_rows + j
                ].astype(BF16)

    held = pl.BlockSpec(memory_space=pltpu.HBM)
    stored = [
        pltpu.with_memory_space_constraint(v, pltpu.HBM)
        for v in (tile_rows, tile_cols, tiles)
    ]
    return pl.pallas_call(
        body,
        out_shape=sds((grid_cols * edge, grid_rows * edge), BF16),
        in_specs=[pl.BlockSpec(memory_space=pltpu.SMEM)] + [held] * 3,
        out_specs=pl.BlockSpec(memory_space=pltpu.VMEM),
        scratch_shapes=[
            pltpu.VMEM((grid_rows * grid_cols, edge, edge), F32),
            pltpu.VMEM((total, edge, edge), BF16),
            pltpu.SMEM((total,), jnp.int32),
            pltpu.SMEM((total,), jnp.int32),
            pltpu.SemaphoreType.DMA((groups + 2,)),
        ],
        compiler_params=pltpu.CompilerParams(vmem_limit_bytes=24 << 20),
        cost_estimate=pl.CostEstimate(
            flops=1 << 24, bytes_accessed=4 * total * edge * edge, transcendentals=0
        ),
        name="build_cell",
    )(tile_counts, *stored)


def swap(value, axis, distance):
    size = lax.axis_size(axis)
    return lax.ppermute(value, axis, [(i, i ^ distance) for i in range(size)])


def swap_corner(value):
    size = lax.axis_size("row") * lax.axis_size("col")
    step = lax.axis_size("col") + 1
    return lax.ppermute(value, ("row", "col"), [(i, i ^ step) for i in range(size)])


def direct_form(
    node_feats,
    degrees,
    self_weight,
    neigh_weight,
    bias,
    tiles,
    tile_rows,
    tile_cols,
    tile_counts,
    out_grad,
):
    grid_rows = lax.axis_size("row")
    grid_cols = lax.axis_size("col")
    half = grid_cols // 2
    n, width = node_feats.shape
    grad_scale = 1.0 / math.sqrt(grid_rows * grid_cols * n)

    feats = [node_feats] + [swap(node_feats, "row", k) for k in range(1, grid_rows)]

    cell = build_cell(
        tile_counts, tile_rows[0, 0], tile_cols[0, 0], tiles[0, 0], grid_rows, grid_cols
    )

    def prepare(x_ref, w_ref, b_ref, d_ref, pre_ref, deg_ref, degrow_ref):
        pre_ref[...] = dot(x_ref[...], w_ref[...]) + b_ref[...]
        line = d_ref[...].astype(F32)
        degrow_ref[...] = line
        deg_ref[...] = jnp.broadcast_to(line, (n, n)).T

    pre, deg, deg_row = call(
        prepare,
        [sds((n, width), F32), sds((n, n), F32), sds((1, n), F32)],
        [node_feats, self_weight, bias.reshape(1, width), degrees.reshape(1, n)],
        "prepare",
    )

    def products(part, cell_ref, *refs):
        *x_refs, out_ref = refs
        stripe = jnp.concatenate([r[...] for r in x_refs], axis=0)
        rows = half * n
        out_ref[...] = dot(cell_ref[part * rows : (part + 1) * rows, :], stripe).astype(
            out_ref.dtype
        )

    work = (half * n * grid_rows * n * width, 1 << 19)
    rows = half * n // 2

    def strip(first):
        def body(cell_ref, *refs):
            *x_refs, out_ref = refs
            stripe = jnp.concatenate([r[...] for r in x_refs], axis=0)
            out_ref[...] = dot(cell_ref[first : first + out_ref.shape[0], :], stripe).astype(
                out_ref.dtype
            )

        return body

    sent_in = []
    for part in (3, 2):
        sent = call(
            strip(part * rows), sds((rows, width), BF16), [cell, *feats], "forward_sent", cost=work
        )
        sent_in.append(swap(sent, "col", 1))
    kept = call(
        strip(0), sds((half * n, width), F32), [cell, *feats], "forward_kept", cost=work
    )

    def pair_far(kept_ref, in_ref, *out_refs):
        total = kept_ref[rows:, :] + in_ref[...].astype(F32)
        for q, ref in enumerate(out_refs):
            ref[...] = total[q * n : (q + 1) * n].astype(BF16)

    def pair_near(kept_ref, in_ref, own_ref, *out_refs):
        total = kept_ref[:rows, :] + in_ref[...].astype(F32)
        own_ref[...] = total[:n]
        for q, ref in enumerate(out_refs):
            ref[...] = total[(q + 1) * n : (q + 2) * n].astype(BF16)

    block = sds((n, width), BF16)
    far_parts = call(pair_far, [block] * (half // 2), [kept, sent_in[0]], "pair_far")
    own_sum, *near_parts = call(
        pair_near,
        [sds((n, width), F32)] + [block] * (half // 2 - 1),
        [kept, sent_in[1]],
        "pair_near",
    )
    parts = [*near_parts, *far_parts]
    parts_in = [swap(part, "col", 2 * (q + 1)) for q, part in enumerate(parts)]

    pad = 16
    piece = width // 2
    small = sds((piece + pad, width), BF16)
    inward = half - 1

    def dense(own_ref, *refs):
        in_refs, refs = refs[:inward], refs[inward:]
        x_ref, pre_ref, deg_ref, degrow_ref, wn_ref, g_ref = refs[:6]
        spread_ref, preact_ref, dpre_ref, *out_refs = refs[6:]
        total = own_ref[...]
        for ref in in_refs:
            total = total + ref[...].astype(F32)
        d = deg_ref[...]
        agg = (total / jnp.concatenate([d] * (width // n), axis=1)).astype(BF16)
        v = pre_ref[...] + dot(agg, wn_ref[...])
        preact_ref[...] = v
        s = jax.nn.sigmoid(v)
        dpre = g_ref[...].astype(F32) * s * (1.0 + v * (1.0 - s))
        dpre_b = dpre.astype(BF16)
        dpre_ref[...] = dpre_b
        line = jnp.broadcast_to(jnp.sum(dpre, axis=0, keepdims=True), (pad, width)).astype(BF16)
        on_first = (lax.axis_index("col") & 1) == 0
        on_left = (lax.axis_index("row") & 1) == 0
        feats_own = x_ref[...]
        mine = jnp.where(on_first, feats_own, agg)
        other = jnp.where(on_first, agg, feats_own)
        for ref, source, left in (
            (out_refs[1], other, on_left),
            (out_refs[2], mine, ~on_left),
            (out_refs[3], other, ~on_left),
            (out_refs[0], mine, on_left),
        ):
            block = jnp.where(left, source[:, :piece], source[:, piece:])
            ref[:piece] = lax.dot_general(
                block, dpre_b, FIRST, preferred_element_type=F32
            ).astype(BF16)
            ref[piece:] = line
        back = lax.dot_general(wn_ref[...], dpre_b, LAST, preferred_element_type=F32)
        spread_ref[...] = (back / degrow_ref[...]).astype(BF16)

    spread, preact, dpre_b, g_own, g_core, g_side, g_corner = call(
        dense,
        [sds((width, n), BF16), sds((n, width), F32), sds((n, width), BF16)] + [small] * 4,
        [
            own_sum,
            *parts_in[::-1],
            node_feats,
            pre,
            deg,
            deg_row,
            neigh_weight,
            out_grad,
        ],
        "dense",
    )
    near = [spread] + [swap(spread, "col", 2 * q) for q in range(1, half)]

    def add_many(*refs):
        *in_refs, out_ref = refs
        vals = [ref[...].astype(F32) for ref in in_refs]
        while len(vals) > 1:
            vals = [vals[i] + vals[i + 1] for i in range(0, len(vals), 2)]
        out_ref[...] = vals[0].astype(BF16)

    g_in = [swap_corner(g_corner), swap(g_side, "row", 1), swap(g_core, "col", 1)]
    g_part = call(add_many, small, [g_own, *g_in[::-1]], "add_corner", after=())
    y_in = [swap(g_part, "row", 2 ** i) for i in range(1, grid_rows.bit_length() - 1)]

    far = [swap(part, "col", 1) for part in near]

    def back_first(cell_ref, *refs):
        *s_refs, out_ref = refs
        left = jnp.concatenate([r[...] for r in s_refs], axis=1)
        out_ref[...] = dot(left, cell_ref[: half * n, :])

    back_a = call(
        back_first, sds((width, grid_rows * n), F32), [cell, *near], "back_first", cost=work
    )

    def back_second(cell_ref, a_ref, *refs):
        s_refs, out_refs = refs[:half], refs[half:]
        left = jnp.concatenate([r[...] for r in s_refs], axis=1)
        total = a_ref[...] + dot(left, cell_ref[half * n :, :])
        out_refs[0][...] = total[:, :n]
        for k in range(1, grid_rows):
            out_refs[k][...] = total[:, k * n : (k + 1) * n].astype(BF16)

    own_back, *back_parts = call(
        back_second,
        [sds((width, n), F32)] + [sds((width, n), BF16)] * (grid_rows - 1),
        [cell, back_a, *far],
        "back_second",
        cost=work,
    )
    back_in = [swap(part, "row", k + 1) for k, part in enumerate(back_parts)]

    def activate(v_ref, w_ref, d_ref, hid_ref, own_ref):
        v = v_ref[...]
        hid_ref[...] = (v * jax.nn.sigmoid(v)).astype(BF16)
        own_ref[...] = lax.dot_general(w_ref[...], d_ref[...], LAST, preferred_element_type=F32)

    hidden, own_grad = call(
        activate,
        [sds((n, width), BF16), sds((width, n), F32)],
        [preact, self_weight, dpre_b],
        "activate",
        after=[own_back],
    )

    def finish(grad_ref, own_ref, *refs):
        *in_refs, out_ref = refs
        total = grad_ref[...] + own_ref[...]
        for ref in in_refs:
            total = total + ref[...].astype(F32)
        out_ref[...] = total.T.astype(BF16)

    feat_grad = call(finish, sds((n, width), BF16), [own_grad, own_back, *back_in], "finish")

    z_part = g_part
    for got in y_in:
        z_part = call(add_many, small, [z_part, got], "add_y", after=near[1:])
    z_in = [swap(z_part, "col", 2 * q) for q in range(1, half)]
    g_piece = call(add_many, small, [z_part, *z_in], "add_z", after=[own_back])
    pieces = g_piece[:piece]
    pieces_in = [swap_corner(pieces), swap(pieces, "row", 1), swap(pieces, "col", 1)]

    def write(parts, hbms, blocks, sems):
        x, c = lax.axis_index("row") & 1, lax.axis_index("col") & 1
        for j, (ref, side, core) in enumerate(parts):
            blocks[j] = ref[:piece].astype(F32) * grad_scale
            base = (x ^ side) * piece
            for which, hbm in enumerate(hbms):

                @pl.when((c ^ core) == which)
                def _():
                    for i in range(0, piece, STRIP):
                        to = pl.ds(pl.multiple_of(base + i, STRIP), STRIP)
                        pltpu.make_async_copy(
                            blocks.at[j, pl.ds(i, STRIP)], hbm.at[to], sems.at[j]
                        ).start()

    def drain(count, hbm, blocks, sems):
        for j in range(count):
            pltpu.make_async_copy(blocks.at[j], hbm.at[pl.ds(0, piece)], sems.at[j]).wait()

    def write_first(a_ref, b_ref, self_hbm, neigh_hbm, bias_hbm, blocks, sems, line):
        line[...] = a_ref[piece : piece + 1].astype(F32) * grad_scale
        copy = pltpu.make_async_copy(line, bias_hbm, sems.at[2])
        copy.start()
        parts = ((a_ref, 0, 0), (b_ref, 0, 1))
        write(parts, (self_hbm, neigh_hbm), blocks, sems)
        drain(2, self_hbm, blocks, sems)
        copy.wait()

    def write_next(core, a_ref, s_ref, n_ref, self_hbm, neigh_hbm, blocks, sems):
        write(((a_ref, 1, core),), (self_hbm, neigh_hbm), blocks, sems)
        drain(1, self_hbm, blocks, sems)

    held, fast = (pl.BlockSpec(memory_space=m) for m in (pltpu.HBM, pltpu.VMEM))
    whole = [sds((width, width), F32)] * 2
    common = dict(
        compiler_params=pltpu.CompilerParams(vmem_limit_bytes=24 << 20),
        cost_estimate=pl.CostEstimate(flops=1 << 20, bytes_accessed=1 << 18, transcendentals=0),
    )
    scratch = [pltpu.VMEM((2, piece, width), F32), pltpu.SemaphoreType.DMA((3,))]
    corner_in, side_in, core_in = pieces_in
    *grads, grad_bias = pl.pallas_call(
        write_first,
        out_shape=whole + [sds((1, width), F32)],
        in_specs=[fast, fast],
        out_specs=[held, held, held],
        scratch_shapes=scratch + [pltpu.VMEM((1, width), F32)],
        name="write_first",
        **common,
    )(g_piece, core_in)
    for core, got in ((1, corner_in), (0, side_in)):
        grads = pl.pallas_call(
            functools.partial(write_next, core),
            out_shape=whole,
            in_specs=[fast, held, held],
            out_specs=[held, held],
            input_output_aliases={1: 0, 2: 1},
            scratch_shapes=scratch,
            name="write_next",
            **common,
        )(got, *grads)
    grad_self, grad_neigh = grads
    return hidden, feat_grad, grad_self, grad_neigh, grad_bias.reshape(width)


def on_device(*args):
    node_feats, tiles = args[0], args[5]
    n, width = node_feats.shape
    grid_rows, grid_cols = lax.axis_size("row"), lax.axis_size("col")
    powers = all(s & (s - 1) == 0 and s >= 2 for s in (grid_rows, grid_cols))
    dense_cell = grid_rows * grid_cols <= tiles.shape[2]
    if powers and dense_cell and n == tiles.shape[-1] and n == 128 and width % 256 == 0:
        return direct_form(*args)
    return general_form(*args)


def solution(mesh):
    placed = (
        P(("row", "col"), None),
        P(("row", "col")),
        P(),
        P(),
        P(),
        P("row", "col", None, None, None),
        P("row", "col", None),
        P("row", "col", None),
        P("row", "col"),
        P(("row", "col"), None),
    )
    return jax.shard_map(
        on_device,
        mesh=mesh,
        in_specs=placed,
        out_specs=(P(("row", "col"), None), P(("row", "col"), None), P(), P(), P()),
        check_vma=False,
    )
```

```python
import functools
import math

import jax
import jax.numpy as jnp
from jax import lax
from jax.experimental import pallas as pl
from jax.experimental.pallas import tpu as pltpu
from jax.sharding import PartitionSpec as P

F32 = jnp.float32
BF16 = jnp.bfloat16
STRIP = 16
LAST = (((1,), (1,)), ((), ()))
FIRST = (((0,), (0,)), ((), ()))


def tile_products(block_vals, near_index, far_index, live_count, source, out_blocks, transposed):
    tile_total = block_vals.shape[0]
    group_size = min(16, tile_total)
    tile_edge = block_vals.shape[-1]
    feat_width = source.shape[-1]
    source_blocks = source.reshape(source.shape[0] // tile_edge, tile_edge, feat_width)
    turn_count = (live_count + group_size - 1) // group_size

    def advance(turn, running):
        first_tile = turn * group_size
        group_vals = lax.dynamic_slice_in_dim(block_vals, first_tile, group_size, 0)
        fetch_index = lax.dynamic_slice_in_dim(far_index, first_tile, group_size, 0)
        place_index = lax.dynamic_slice_in_dim(near_index, first_tile, group_size, 0)
        picked = source_blocks[fetch_index]
        if transposed:
            products = jnp.einsum("kab,kaf->kbf", group_vals, picked, preferred_element_type=F32)
        else:
            products = jnp.einsum("kab,kbf->kaf", group_vals, picked, preferred_element_type=F32)
        ordinal = first_tile + jnp.arange(group_size)
        active = ordinal < live_count
        table = (
            (place_index[:, None] == jnp.arange(out_blocks)[None, :]) & active[:, None]
        ).astype(F32)
        return running + jnp.einsum("kl,kaf->laf", table, products)

    initial = jnp.zeros((out_blocks, tile_edge, feat_width), F32)
    result = lax.fori_loop(0, turn_count, advance, initial)
    return result.reshape(out_blocks * tile_edge, feat_width)


def general_form(
    node_feats,
    degrees,
    self_weight,
    neigh_weight,
    bias,
    tiles,
    tile_rows,
    tile_cols,
    tile_counts,
    out_grad,
):
    grid_rows = lax.axis_size("row")
    grid_cols = lax.axis_size("col")
    per_device = node_feats.shape[0]
    tile_edge = tiles.shape[-1]
    block_vals = tiles[0, 0]
    block_rows = tile_rows[0, 0]
    block_cols = tile_cols[0, 0]
    live_count = tile_counts[0, 0]
    row_blocks = grid_cols * per_device // tile_edge
    col_blocks = grid_rows * per_device // tile_edge
    stripe = lax.all_gather(node_feats, "row", axis=0, tiled=True)
    partial_value = tile_products(
        block_vals, block_rows, block_cols, live_count, stripe, row_blocks, False
    )
    summed = lax.psum_scatter(
        partial_value.astype(BF16), "col", scatter_dimension=0, tiled=True
    ).astype(F32)
    degree_col = degrees.astype(F32)[:, None]
    aggregate = (summed / degree_col).astype(BF16)
    preact = (
        jnp.dot(node_feats, self_weight, preferred_element_type=F32)
        + jnp.dot(aggregate, neigh_weight, preferred_element_type=F32)
        + bias
    )
    hidden = jax.nn.silu(preact).astype(BF16)
    sigmoid_val = jax.nn.sigmoid(preact)
    dpre = out_grad.astype(F32) * sigmoid_val * (1.0 + preact * (1.0 - sigmoid_val))
    dpre_b = dpre.astype(BF16)
    self_term = lax.dot_general(node_feats, dpre_b, FIRST, preferred_element_type=F32)
    neigh_term = lax.dot_general(aggregate, dpre_b, FIRST, preferred_element_type=F32)
    bias_term = jnp.sum(dpre, axis=0)
    self_total, neigh_total, bias_total = lax.psum(
        (self_term, neigh_term, bias_term), ("row", "col")
    )
    grad_scale = 1.0 / math.sqrt(grid_rows * grid_cols * per_device)
    back_agg = lax.dot_general(dpre_b, neigh_weight, LAST, preferred_element_type=F32)
    spread = (back_agg / degree_col).astype(BF16)
    row_stripe = lax.all_gather(spread, "col", axis=0, tiled=True)
    back_partial = tile_products(
        block_vals, block_cols, block_rows, live_count, row_stripe, col_blocks, True
    )
    neighbour_grad = lax.psum_scatter(
        back_partial.astype(BF16), "row", scatter_dimension=0, tiled=True
    ).astype(F32)
    own_grad = lax.dot_general(dpre_b, self_weight, LAST, preferred_element_type=F32)
    feat_grad = (own_grad + neighbour_grad).astype(BF16)
    return (
        hidden,
        feat_grad,
        self_total * grad_scale,
        neigh_total * grad_scale,
        bias_total * grad_scale,
    )


def sds(shape, dtype):
    return jax.ShapeDtypeStruct(shape, dtype)


def call(kernel, outs, args, name, after=(), cost=None):
    single = not isinstance(outs, (list, tuple))
    outs = [outs] if single else list(outs)
    count = len(args)
    in_specs = [pl.BlockSpec(memory_space=pltpu.VMEM)] * count
    in_specs += [pl.BlockSpec(memory_space=pl.ANY)] * len(after)

    def body(*refs):
        kernel(*refs[:count], *refs[count + len(after) :])

    flops, moved = cost or (1 << 20, 1 << 18)
    result = pl.pallas_call(
        body,
        out_shape=outs,
        in_specs=in_specs,
        out_specs=[pl.BlockSpec(memory_space=pltpu.VMEM)] * len(outs),
        compiler_params=pltpu.CompilerParams(vmem_limit_bytes=24 << 20),
        cost_estimate=pl.CostEstimate(flops=flops, bytes_accessed=moved, transcendentals=0),
        name=name,
    )(*args, *after)
    return result[0] if single else result


def dot(a, b):
    return jnp.dot(a, b, preferred_element_type=F32)


def build_cell(tile_counts, tile_rows, tile_cols, tiles, grid_rows, grid_cols):
    total, edge = tiles.shape[0], tiles.shape[-1]
    group = 16 if total % 16 == 0 else total
    groups = total // group
    half = grid_cols // 2

    def body(*refs):
        count_ref, rows_hbm, cols_hbm, tiles_hbm, cell_ref = refs[:5]
        sums, vals, rows, cols, sems = refs[5:]
        copies = [
            pltpu.make_async_copy(rows_hbm, rows, sems.at[groups]),
            pltpu.make_async_copy(cols_hbm, cols, sems.at[groups + 1]),
        ]
        for g in range(groups):
            span = pl.ds(g * group, group)
            copies.append(pltpu.make_async_copy(tiles_hbm.at[span], vals.at[span], sems.at[g]))
        for copy in copies:
            copy.start()
        sums[...] = jnp.zeros_like(sums)
        my_row, my_col = lax.axis_index("row"), lax.axis_index("col")

        def add_tile(k, carry):
            near = rows[k] ^ my_col
            far = cols[k] ^ my_row
            slot = ((near >> 1) + half * (near & 1)) * grid_rows + far
            sums[slot] += vals[k].astype(F32)
            return carry

        copies[0].wait()
        copies[1].wait()
        count = count_ref[0, 0]
        for g in range(groups):
            copies[2 + g].wait()
            lax.fori_loop(g * group, jnp.clip(count, g * group, (g + 1) * group), add_tile, 0)
        for i in range(grid_cols):
            for j in range(grid_rows):
                cell_ref[i * edge : (i + 1) * edge, j * edge : (j + 1) * edge] = sums[
                    i * grid_rows + j
                ].astype(BF16)

    held = pl.BlockSpec(memory_space=pltpu.HBM)
    stored = [
        pltpu.with_memory_space_constraint(v, pltpu.HBM)
        for v in (tile_rows, tile_cols, tiles)
    ]
    return pl.pallas_call(
        body,
        out_shape=sds((grid_cols * edge, grid_rows * edge), BF16),
        in_specs=[pl.BlockSpec(memory_space=pltpu.SMEM)] + [held] * 3,
        out_specs=pl.BlockSpec(memory_space=pltpu.VMEM),
        scratch_shapes=[
            pltpu.VMEM((grid_rows * grid_cols, edge, edge), F32),
            pltpu.VMEM((total, edge, edge), BF16),
            pltpu.SMEM((total,), jnp.int32),
            pltpu.SMEM((total,), jnp.int32),
            pltpu.SemaphoreType.DMA((groups + 2,)),
        ],
        compiler_params=pltpu.CompilerParams(vmem_limit_bytes=24 << 20),
        cost_estimate=pl.CostEstimate(
            flops=1 << 24, bytes_accessed=4 * total * edge * edge, transcendentals=0
        ),
        name="build_cell",
    )(tile_counts, *stored)


def swap(value, axis, distance):
    size = lax.axis_size(axis)
    return lax.ppermute(value, axis, [(i, i ^ distance) for i in range(size)])


def swap_corner(value):
    size = lax.axis_size("row") * lax.axis_size("col")
    step = lax.axis_size("col") + 1
    return lax.ppermute(value, ("row", "col"), [(i, i ^ step) for i in range(size)])


def direct_form(
    node_feats,
    degrees,
    self_weight,
    neigh_weight,
    bias,
    tiles,
    tile_rows,
    tile_cols,
    tile_counts,
    out_grad,
):
    grid_rows = lax.axis_size("row")
    grid_cols = lax.axis_size("col")
    half = grid_cols // 2
    n, width = node_feats.shape
    grad_scale = 1.0 / math.sqrt(grid_rows * grid_cols * n)

    feats = [node_feats] + [swap(node_feats, "row", k) for k in range(1, grid_rows)]

    cell = build_cell(
        tile_counts, tile_rows[0, 0], tile_cols[0, 0], tiles[0, 0], grid_rows, grid_cols
    )

    def prepare(x_ref, w_ref, b_ref, d_ref, pre_ref, deg_ref, degrow_ref):
        pre_ref[...] = dot(x_ref[...], w_ref[...]) + b_ref[...]
        line = d_ref[...].astype(F32)
        degrow_ref[...] = line
        deg_ref[...] = jnp.broadcast_to(line, (n, n)).T

    pre, deg, deg_row = call(
        prepare,
        [sds((n, width), F32), sds((n, n), F32), sds((1, n), F32)],
        [node_feats, self_weight, bias.reshape(1, width), degrees.reshape(1, n)],
        "prepare",
    )

    def products(part, cell_ref, *refs):
        *x_refs, out_ref = refs
        stripe = jnp.concatenate([r[...] for r in x_refs], axis=0)
        rows = half * n
        out_ref[...] = dot(cell_ref[part * rows : (part + 1) * rows, :], stripe).astype(
            out_ref.dtype
        )

    work = (half * n * grid_rows * n * width, 1 << 19)
    rows = half * n // 2

    def strip(first):
        def body(cell_ref, *refs):
            *x_refs, out_ref = refs
            stripe = jnp.concatenate([r[...] for r in x_refs], axis=0)
            out_ref[...] = dot(cell_ref[first : first + out_ref.shape[0], :], stripe).astype(
                out_ref.dtype
            )

        return body

    sent_in = []
    for part in (3, 2):
        sent = call(
            strip(part * rows), sds((rows, width), BF16), [cell, *feats], "forward_sent", cost=work
        )
        sent_in.append(swap(sent, "col", 1))
    kept = call(
        strip(0), sds((half * n, width), F32), [cell, *feats], "forward_kept", cost=work
    )

    def pair_far(kept_ref, in_ref, *out_refs):
        total = kept_ref[rows:, :] + in_ref[...].astype(F32)
        for q, ref in enumerate(out_refs):
            ref[...] = total[q * n : (q + 1) * n].astype(BF16)

    def pair_near(kept_ref, in_ref, own_ref, *out_refs):
        total = kept_ref[:rows, :] + in_ref[...].astype(F32)
        own_ref[...] = total[:n]
        for q, ref in enumerate(out_refs):
            ref[...] = total[(q + 1) * n : (q + 2) * n].astype(BF16)

    block = sds((n, width), BF16)
    far_parts = call(pair_far, [block] * (half // 2), [kept, sent_in[0]], "pair_far")
    own_sum, *near_parts = call(
        pair_near,
        [sds((n, width), F32)] + [block] * (half // 2 - 1),
        [kept, sent_in[1]],
        "pair_near",
    )
    parts = [*near_parts, *far_parts]
    parts_in = [swap(part, "col", 2 * (q + 1)) for q, part in enumerate(parts)]

    pad = 8
    piece = width // 2
    small = sds((piece + pad, width), BF16)
    inward = half - 1

    def dense(own_ref, *refs):
        in_refs, refs = refs[:inward], refs[inward:]
        x_ref, pre_ref, deg_ref, degrow_ref, wn_ref, g_ref = refs[:6]
        spread_ref, preact_ref, dpre_ref, *out_refs = refs[6:]
        total = own_ref[...]
        for ref in in_refs:
            total = total + ref[...].astype(F32)
        d = deg_ref[...]
        agg = (total / jnp.concatenate([d] * (width // n), axis=1)).astype(BF16)
        v = pre_ref[...] + dot(agg, wn_ref[...])
        preact_ref[...] = v
        s = jax.nn.sigmoid(v)
        dpre = g_ref[...].astype(F32) * s * (1.0 + v * (1.0 - s))
        dpre_b = dpre.astype(BF16)
        dpre_ref[...] = dpre_b
        line = jnp.broadcast_to(jnp.sum(dpre, axis=0, keepdims=True), (pad, width)).astype(BF16)
        on_first = (lax.axis_index("col") & 1) == 0
        on_left = (lax.axis_index("row") & 1) == 0
        feats_own = x_ref[...]
        mine = jnp.where(on_first, feats_own, agg)
        other = jnp.where(on_first, agg, feats_own)
        for ref, source, left in (
            (out_refs[1], other, on_left),
            (out_refs[2], mine, ~on_left),
            (out_refs[3], other, ~on_left),
            (out_refs[0], mine, on_left),
        ):
            block = jnp.where(left, source[:, :piece], source[:, piece:])
            ref[:piece] = lax.dot_general(
                block, dpre_b, FIRST, preferred_element_type=F32
            ).astype(BF16)
            ref[piece:] = line
        back = lax.dot_general(wn_ref[...], dpre_b, LAST, preferred_element_type=F32)
        spread_ref[...] = (back / degrow_ref[...]).astype(BF16)

    spread, preact, dpre_b, g_own, g_core, g_side, g_corner = call(
        dense,
        [sds((width, n), BF16), sds((n, width), F32), sds((n, width), BF16)] + [small] * 4,
        [
            own_sum,
            *parts_in[::-1],
            node_feats,
            pre,
            deg,
            deg_row,
            neigh_weight,
            out_grad,
        ],
        "dense",
    )
    near = [spread] + [swap(spread, "col", 2 * q) for q in range(1, half)]

    def add_many(*refs):
        *in_refs, out_ref = refs
        vals = [ref[...].astype(F32) for ref in in_refs]
        while len(vals) > 1:
            vals = [vals[i] + vals[i + 1] for i in range(0, len(vals), 2)]
        out_ref[...] = vals[0].astype(BF16)

    g_in = [swap_corner(g_corner), swap(g_side, "row", 1), swap(g_core, "col", 1)]
    g_part = call(add_many, small, [g_own, *g_in[::-1]], "add_corner", after=())
    y_in = [swap(g_part, "row", 2 ** i) for i in range(1, grid_rows.bit_length() - 1)]

    far = [swap(part, "col", 1) for part in near]

    def back_first(cell_ref, *refs):
        *s_refs, out_ref = refs
        left = jnp.concatenate([r[...] for r in s_refs], axis=1)
        out_ref[...] = dot(left, cell_ref[: half * n, :])

    back_a = call(
        back_first, sds((width, grid_rows * n), F32), [cell, *near], "back_first", cost=work
    )

    def back_second(cell_ref, a_ref, *refs):
        s_refs, out_refs = refs[:half], refs[half:]
        left = jnp.concatenate([r[...] for r in s_refs], axis=1)
        total = a_ref[...] + dot(left, cell_ref[half * n :, :])
        out_refs[0][...] = total[:, :n]
        for k in range(1, grid_rows):
            out_refs[k][...] = total[:, k * n : (k + 1) * n].astype(BF16)

    own_back, *back_parts = call(
        back_second,
        [sds((width, n), F32)] + [sds((width, n), BF16)] * (grid_rows - 1),
        [cell, back_a, *far],
        "back_second",
        cost=work,
    )
    back_in = [swap(part, "row", k + 1) for k, part in enumerate(back_parts)]

    def activate(v_ref, w_ref, d_ref, hid_ref, own_ref):
        v = v_ref[...]
        hid_ref[...] = (v * jax.nn.sigmoid(v)).astype(BF16)
        own_ref[...] = lax.dot_general(w_ref[...], d_ref[...], LAST, preferred_element_type=F32)

    hidden, own_grad = call(
        activate,
        [sds((n, width), BF16), sds((width, n), F32)],
        [preact, self_weight, dpre_b],
        "activate",
        after=[own_back],
    )

    def finish(grad_ref, own_ref, *refs):
        *in_refs, out_ref = refs
        total = grad_ref[...] + own_ref[...]
        for ref in in_refs:
            total = total + ref[...].astype(F32)
        out_ref[...] = total.T.astype(BF16)

    feat_grad = call(finish, sds((n, width), BF16), [own_grad, own_back, *back_in], "finish")

    z_part = g_part
    for got in y_in:
        z_part = call(add_many, small, [z_part, got], "add_y", after=near[1:])
    z_in = [swap(z_part, "col", 2 * q) for q in range(1, half)]
    g_piece = call(add_many, small, [z_part, *z_in], "add_z", after=[own_back])
    pieces = g_piece[:piece]
    pieces_in = [swap_corner(pieces), swap(pieces, "row", 1), swap(pieces, "col", 1)]

    def write(parts, hbms, blocks, sems):
        x, c = lax.axis_index("row") & 1, lax.axis_index("col") & 1
        for j, (ref, side, core) in enumerate(parts):
            blocks[j] = ref[:piece].astype(F32) * grad_scale
            base = (x ^ side) * piece
            for which, hbm in enumerate(hbms):

                @pl.when((c ^ core) == which)
                def _():
                    for i in range(0, piece, STRIP):
                        to = pl.ds(pl.multiple_of(base + i, STRIP), STRIP)
                        pltpu.make_async_copy(
                            blocks.at[j, pl.ds(i, STRIP)], hbm.at[to], sems.at[j]
                        ).start()

    def drain(count, hbm, blocks, sems):
        for j in range(count):
            pltpu.make_async_copy(blocks.at[j], hbm.at[pl.ds(0, piece)], sems.at[j]).wait()

    def write_first(a_ref, b_ref, self_hbm, neigh_hbm, bias_hbm, blocks, sems, line):
        line[...] = a_ref[piece : piece + 1].astype(F32) * grad_scale
        copy = pltpu.make_async_copy(line, bias_hbm, sems.at[2])
        copy.start()
        parts = ((a_ref, 0, 0), (b_ref, 0, 1))
        write(parts, (self_hbm, neigh_hbm), blocks, sems)
        drain(2, self_hbm, blocks, sems)
        copy.wait()

    def write_next(core, a_ref, s_ref, n_ref, self_hbm, neigh_hbm, blocks, sems):
        write(((a_ref, 1, core),), (self_hbm, neigh_hbm), blocks, sems)
        drain(1, self_hbm, blocks, sems)

    held, fast = (pl.BlockSpec(memory_space=m) for m in (pltpu.HBM, pltpu.VMEM))
    whole = [sds((width, width), F32)] * 2
    common = dict(
        compiler_params=pltpu.CompilerParams(vmem_limit_bytes=24 << 20),
        cost_estimate=pl.CostEstimate(flops=1 << 20, bytes_accessed=1 << 18, transcendentals=0),
    )
    scratch = [pltpu.VMEM((2, piece, width), F32), pltpu.SemaphoreType.DMA((3,))]
    corner_in, side_in, core_in = pieces_in
    *grads, grad_bias = pl.pallas_call(
        write_first,
        out_shape=whole + [sds((1, width), F32)],
        in_specs=[fast, fast],
        out_specs=[held, held, held],
        scratch_shapes=scratch + [pltpu.VMEM((1, width), F32)],
        name="write_first",
        **common,
    )(g_piece, core_in)
    for core, got in ((1, corner_in), (0, side_in)):
        grads = pl.pallas_call(
            functools.partial(write_next, core),
            out_shape=whole,
            in_specs=[fast, held, held],
            out_specs=[held, held],
            input_output_aliases={1: 0, 2: 1},
            scratch_shapes=scratch,
            name="write_next",
            **common,
        )(got, *grads)
    grad_self, grad_neigh = grads
    return hidden, feat_grad, grad_self, grad_neigh, grad_bias.reshape(width)


def on_device(*args):
    node_feats, tiles = args[0], args[5]
    n, width = node_feats.shape
    grid_rows, grid_cols = lax.axis_size("row"), lax.axis_size("col")
    powers = all(s & (s - 1) == 0 and s >= 2 for s in (grid_rows, grid_cols))
    dense_cell = grid_rows * grid_cols <= tiles.shape[2]
    if powers and dense_cell and n == tiles.shape[-1] and n == 128 and width % 256 == 0:
        return direct_form(*args)
    return general_form(*args)


def solution(mesh):
    placed = (
        P(("row", "col"), None),
        P(("row", "col")),
        P(),
        P(),
        P(),
        P("row", "col", None, None, None),
        P("row", "col", None),
        P("row", "col", None),
        P("row", "col"),
        P(("row", "col"), None),
    )
    return jax.shard_map(
        on_device,
        mesh=mesh,
        in_specs=placed,
        out_specs=(P(("row", "col"), None), P(("row", "col"), None), P(), P(), P()),
        check_vma=False,
    )
```
